32 devices in a mesh: seq: 8 (over y, x, core), wshard: 4 (over z).
Axes of the slice: x: 2, y: 2, z: 4, core: 2. Of those that a mesh axis runs over, the one named last changes fastest.
Arguments:
- block_in: bfloat16 [4, 1024, 2560], P('wshard', 'seq'), may hold values from -6 to 6
- cotangent: bfloat16 [4, 1024, 2560], P('wshard', 'seq'), may hold values from -6 to 6
- w_x: bfloat16 [2560, 2560], P('wshard'), may hold values from -0.125 to 0.125
- w_y: bfloat16 [2560, 2560], P('wshard'), may hold values from -0.125 to 0.125
- w_out: bfloat16 [2560, 2560], P('wshard'), may hold values from -0.125 to 0.125
- w_gate: bfloat16 [7680, 2560], P('wshard'), may hold values from -0.125 to 0.125
- w_up: bfloat16 [7680, 2560], P('wshard'), may hold values from -0.125 to 0.125
- w_down: bfloat16 [7680, 2560], P('wshard'), may hold values from -0.0625 to 0.0625
- norm1_gain: bfloat16 [2560], P('wshard'), may hold values from 0.099609375 to 1.8984375
- norm2_gain: bfloat16 [2560], P('wshard'), may hold values from 0.099609375 to 1.8984375
- conv_weight: bfloat16 [4, 2560], P(None, 'wshard'), may hold values from -3 to 3
- conv_bias: bfloat16 [2560], P('wshard'), may hold values from -3 to 3
- gate_weight: bfloat16 [2, 10, 256, 256], P(None, None, 'wshard'), may hold values from -0.375 to 0.375
- gate_bias: bfloat16 [2, 2560], P(None, 'wshard'), may hold values from -4 to 4
- decay_param: bfloat16 [2560], P('wshard'), may hold values from 5 to 11
Outputs:
- block_out: bfloat16 [4, 1024, 2560], P('wshard', 'seq')
- grad_input: float32 [4, 1024, 2560], P('wshard', 'seq')
- grad_w_x: float32 [2560, 2560], P('wshard', 'seq')
- grad_w_y: float32 [2560, 2560], P('wshard', 'seq')
- grad_w_out: float32 [2560, 2560], P('wshard', 'seq')
- grad_w_gate: float32 [7680, 2560], P('wshard', 'seq')
- grad_w_up: float32 [7680, 2560], P('wshard', 'seq')
- grad_w_down: float32 [7680, 2560], P('wshard', 'seq')
- grad_norm1: float32 [2560], P('wshard')
- grad_norm2: float32 [2560], P('wshard')
- grad_conv_weight: float32 [4, 2560], P(None, 'wshard')
- grad_conv_bias: float32 [2560], P('wshard')
- grad_gate_weight: float32 [2, 10, 256, 256], P(None, None, 'wshard')
- grad_gate_bias: float32 [2, 2560], P(None, 'wshard')
- grad_decay: float32 [2560], P('wshard')
The draws below stay inside these ranges and needn't reach their ends.
All inputs are finite; a program needn't handle non-finite values.
Results may differ from the reference program's by a relative error of at most 0.019.
Values may be sent and summed in bfloat16 or wider, within the bound.
No kernel may reach another device: no remote copies, remote signals or barrier semaphores. Data moves between devices by JAX's collectives and lax.ppermute only.
A program may use at most 768 MiB of HBM per device.

```python
import jax
import jax.numpy as jnp
from jax import lax

D = 2560
FF = 7680
HEADS = 10
BLOCK = 256
LRU_WIDTH = 2560
CONV = 4
SCAN_BLOCK = 32
SEQ_LEN = 1024
BATCH = 4


def shard_levels(stream_key, extent, pieces, smallest, top_value):
    def one(position, parts):
        heights = jax.random.uniform(jax.random.fold_in(jax.random.fold_in(stream_key, 6), position), (parts,), jnp.float32, smallest / len(pieces), top_value / len(pieces))
        return jnp.repeat(jnp.exp(heights), extent[position] // parts).reshape((-1,) + (1,) * (len(extent) - position - 1))

    level = one(*pieces[0])
    for cut in pieces[1:]:
        level = level * one(*cut)
    return level


def normal_values(stream_key, extent, scale, most, pieces=(), kind=jnp.bfloat16):
    values = jax.random.normal(stream_key, extent, jnp.float32) * scale
    if len(pieces) > 0:
        values = shard_levels(stream_key, extent, pieces, -0.22, 0.18) * values
    return jnp.clip(values, min=-most, max=most).astype(kind)


def setup_inputs(seed: int = 0) -> dict:
    streams_of = jax.random.split(jax.random.key(seed), 16)
    block_in = normal_values(streams_of[0], (BATCH, SEQ_LEN, D), 1.0, 6.0, ((0, 4), (1, 8)))
    cotangent = normal_values(streams_of[1], (BATCH, SEQ_LEN, D), 1.0, 6.0, ((0, 4), (1, 8)))
    w_x = normal_values(streams_of[2], (LRU_WIDTH, D), D ** -0.5, 0.125, ((0, 4),))
    w_y = normal_values(streams_of[3], (LRU_WIDTH, D), D ** -0.5, 0.125, ((0, 4),))
    w_out = normal_values(streams_of[4], (LRU_WIDTH, D), LRU_WIDTH ** -0.5, 0.125, ((0, 4),))
    w_gate = normal_values(streams_of[5], (FF, D), D ** -0.5, 0.125, ((0, 4),))
    w_up = normal_values(streams_of[6], (FF, D), D ** -0.5, 0.125, ((0, 4),))
    w_down = normal_values(streams_of[7], (FF, D), FF ** -0.5, 0.0625, ((0, 4),))
    norm1_gain = jnp.clip(1.0 + 0.18 * jax.random.normal(streams_of[8], (D,), jnp.float32), 0.099609375, 1.8984375).astype(jnp.bfloat16)
    norm2_gain = jnp.clip(1.0 + 0.18 * jax.random.normal(streams_of[9], (D,), jnp.float32), 0.099609375, 1.8984375).astype(jnp.bfloat16)
    conv_weight = normal_values(streams_of[10], (CONV, LRU_WIDTH), 0.5, 3.0, ((1, 4),))
    conv_bias = normal_values(streams_of[11], (LRU_WIDTH,), 0.5, 3.0, ((0, 4),))
    gate_weight = normal_values(streams_of[12], (2, HEADS, BLOCK, BLOCK), BLOCK ** -0.5, 0.375, ((2, 4),))
    gate_bias = normal_values(streams_of[13], (2, LRU_WIDTH), 1.0, 4.0, ((1, 4),))
    decay_param = jnp.clip(5.0 + 6.0 * jax.random.uniform(streams_of[14], (LRU_WIDTH,), jnp.float32) ** shard_levels(streams_of[14], (LRU_WIDTH,), ((0, 4),), -0.2, 0.2), 5.0, 11.0).astype(jnp.bfloat16)
    return dict(block_in=block_in, cotangent=cotangent, w_x=w_x, w_y=w_y, w_out=w_out, w_gate=w_gate, w_up=w_up, w_down=w_down, norm1_gain=norm1_gain, norm2_gain=norm2_gain, conv_weight=conv_weight, conv_bias=conv_bias, gate_weight=gate_weight, gate_bias=gate_bias, decay_param=decay_param)


EPS = 1e-06
DECAY_SCALE = 8.0
HIGH = lax.Precision.HIGHEST

@jax.custom_vjp
def low(v):
    return lax.optimization_barrier(v.astype(jnp.bfloat16)).astype(jnp.float32)

@jax.custom_vjp
def low_back(v):
    return v

def low_keep(v):
    return (low(v), None)

def low_pass(kept, grad):
    return (grad,)

def back_keep(v):
    return (v, None)

def back_low(kept, grad):
    return (low(grad),)
low.defvjp(low_keep, low_pass)
low_back.defvjp(back_keep, back_low)

def rms_norm(values, gain):
    return values * lax.rsqrt(lax.optimization_barrier(jnp.mean(values * values, axis=-1, keepdims=True)) + EPS) * gain

def gate_heads(inputs, weights):
    rows = inputs.shape[0]
    split = inputs.reshape(rows, HEADS, BLOCK)
    return jnp.einsum('shi,hio->sho', split, weights, precision=HIGH).reshape(rows, HEADS * BLOCK)

def linear_scan(log_decay, inputs):
    length, width = inputs.shape
    count = length // SCAN_BLOCK
    places = jnp.arange(SCAN_BLOCK)
    mask = places[:, None] >= places[None, :]

    def step(carry, pair):
        decay_block, value_block = pair
        cumul = jnp.cumsum(decay_block, axis=0)
        spread = cumul[:, None, :] - cumul[None, :, :]
        weights = jnp.exp(jnp.where(mask[:, :, None], spread, -1e+30))
        result = jnp.einsum('tsw,sw->tw', weights, value_block, precision=HIGH) + jnp.exp(cumul) * carry[None, :]
        return (result[-1], result)
    _, outs = lax.scan(jax.checkpoint(step), jnp.zeros((width,), jnp.float32), (log_decay.reshape(count, SCAN_BLOCK, width), inputs.reshape(count, SCAN_BLOCK, width)))
    return outs.reshape(length, width)

def block_forward(params, inputs):
    w_x, w_y, w_out, w_gate, w_up, w_down, gain_one, gain_two, conv_weight, conv_bias, gate_weight, gate_bias, decay_param = params
    length = inputs.shape[0]
    normed_one = low(rms_norm(inputs, gain_one))
    branch_x = low_back(low(jnp.dot(normed_one, w_x.T, precision=HIGH, preferred_element_type=jnp.float32)))
    branch_y = low_back(jnp.dot(normed_one, w_y.T, precision=HIGH, preferred_element_type=jnp.float32))
    padded = jnp.concatenate([jnp.zeros((CONV - 1, branch_x.shape[1]), jnp.float32), branch_x], axis=0)
    conv = conv_bias
    for tap in range(CONV):
        conv = conv + conv_weight[tap] * padded[CONV - 1 - tap:CONV - 1 - tap + length]
    conv_low = low(conv)
    logit_rec = low_back(gate_heads(conv_low, gate_weight[0]) + gate_bias[0])
    logit_in = low_back(gate_heads(conv_low, gate_weight[1]) + gate_bias[1])
    log_decay = low_back(-DECAY_SCALE * jax.nn.softplus(-decay_param) * jax.nn.sigmoid(logit_rec))
    scan_in = low_back(conv * jax.nn.sigmoid(logit_in))
    state = linear_scan(log_decay, jnp.sqrt(-jnp.expm1(2.0 * log_decay)) * scan_in)
    state_low = low_back(low(state))
    mixed = low(jax.nn.gelu(branch_y, approximate=True) * state_low)
    residual = inputs + low_back(jnp.dot(mixed, w_out, precision=HIGH, preferred_element_type=jnp.float32))
    normed_two = low(rms_norm(residual, gain_two))
    gate = low_back(jnp.dot(normed_two, w_gate.T, precision=HIGH, preferred_element_type=jnp.float32))
    up = low_back(jnp.dot(normed_two, w_up.T, precision=HIGH, preferred_element_type=jnp.float32))
    activ = low(jax.nn.gelu(gate, approximate=True) * up)
    return residual + low_back(jnp.dot(activ, w_down, precision=HIGH, preferred_element_type=jnp.float32))

def reference(block_in, cotangent, w_x, w_y, w_out, w_gate, w_up, w_down, norm1_gain, norm2_gain, conv_weight, conv_bias, gate_weight, gate_bias, decay_param):
    params = tuple((p.astype(jnp.float32) for p in (w_x, w_y, w_out, w_gate, w_up, w_down, norm1_gain, norm2_gain, conv_weight, conv_bias, gate_weight, gate_bias, decay_param)))

    def one_sequence(carry, pair):
        inputs, grad_out = pair
        output, pull = jax.vjp(block_forward, params, inputs.astype(jnp.float32))
        grads, grad_in = pull(grad_out.astype(jnp.float32))
        carry = jax.tree.map(lambda left, right: left + right, carry, grads)
        return (carry, (output.astype(jnp.bfloat16), grad_in))
    zeros = jax.tree.map(jnp.zeros_like, params)
    total, (outputs, grad_inputs) = lax.scan(one_sequence, zeros, (block_in, cotangent))
    return (outputs, grad_inputs, total[0], total[1], total[2], total[3], total[4], total[5], total[6], total[7], total[8], total[9], total[10], total[11], total[12])
```

```python
import functools

import jax
import jax.numpy as jnp
from jax import lax
from jax.experimental import pallas as pl
from jax.experimental.pallas import tpu as pltpu
from jax.sharding import PartitionSpec as P

EPS = 1e-06
DECAY_SCALE = 8.0
HALF = 128
GELU_C = 0.7978845608028654
GELU_K = 0.044715
F32 = jnp.float32
BF16 = jnp.bfloat16


def relay_gather(part, axis="wshard"):
    count = lax.axis_size(axis)
    place = lax.axis_index(axis)
    up = down = part
    ups, downs = [part], [part]
    for k in range(1, count):
        up = lax.ppermute(up, axis, [(i, i + 1) for i in range(k - 1, count - 1)])
        down = lax.ppermute(down, axis, [(i + 1, i) for i in range(count - k)])
        ups.append(up)
        downs.append(down)
    return [part] + [jnp.where(place >= k, ups[k], downs[count - k]) for k in range(1, count)]


def relay_scatter(slots, axis="wshard"):
    count = lax.axis_size(axis)
    up = down = None
    for k in range(1, count):
        out_up = slots[k] if up is None else slots[k] + up.astype(F32)
        out_down = slots[count - k] if down is None else slots[count - k] + down.astype(F32)
        up = lax.ppermute(out_up.astype(BF16), axis, [(i, i + 1) for i in range(k)])
        down = lax.ppermute(
            out_down.astype(BF16), axis, [(i + 1, i) for i in range(count - 1 - k, count - 1)]
        )
    return slots[0] + up.astype(F32) + down.astype(F32)


def exchange_pair(value, axis, bit):
    count = lax.axis_size(axis)
    return lax.ppermute(value, axis, [(i, i ^ bit) for i in range(count)])


def bits_of(count):
    return [1 << i for i in range(count.bit_length() - 1)]


def sum_all(value, axis):
    for bit in bits_of(lax.axis_size(axis)):
        value = value + exchange_pair(value, axis, bit)
    return value


def from_slots(slots, axis="wshard"):
    count = lax.axis_size(axis)
    place = lax.axis_index(axis)
    back = jnp.stack(slots[::-1] + slots[::-1])
    return lax.dynamic_slice_in_dim(back, count - 1 - place, count, 0)


def all_parts(part, axis="wshard"):
    count = lax.axis_size(axis)
    slots = [part] + [
        lax.ppermute(part, axis, [(i, (i + k) % count) for i in range(count)])
        for k in range(1, count)
    ]
    return from_slots(slots, axis)


def swap_parts(parts, axis="wshard"):
    count = lax.axis_size(axis)
    place = lax.axis_index(axis)
    slots = []
    for k in range(count):
        mine = lax.dynamic_index_in_dim(parts, (place + k) % count, 0, keepdims=False)
        if k:
            mine = lax.ppermute(mine, axis, [(i, (i + k) % count) for i in range(count)])
        slots.append(mine)
    return from_slots(slots, axis)


def relative_order(count, order):
    offsets = [0]
    for bit in reversed(order):
        offsets = offsets + [o | bit for o in offsets]
    return offsets


def xor_columns(value, order, axis="seq"):
    count = lax.axis_size(axis)
    place = lax.axis_index(axis)
    width = value.shape[1] // count
    return jnp.concatenate(
        [
            lax.dynamic_slice_in_dim(value, (place ^ offset) * width, width, 1)
            for offset in relative_order(count, order)
        ],
        axis=1,
    )


def halving_grad(left, right, order, axis="seq"):
    rows = left.shape[1]
    size = right.shape[1]
    held = []

    def part(lo, hi):
        total = lax.dot_general(
            left, right[:, lo:hi], (((0,), (0,)), ((), ())), preferred_element_type=F32
        )
        for piece in held:
            total = total + piece[:, lo:hi].astype(F32)
        return total

    for bit in order:
        half = size // 2
        held.append(exchange_pair(part(half, size).astype(BF16), axis, bit))
        size = half
    return part(0, size)


def expm1_neg(v):
    poly = 1.0 + v / 9.0
    for n in range(8, 1, -1):
        poly = 1.0 + poly * v / float(n)
    return jnp.where(v > -0.5, v * poly, jnp.exp(v) - 1.0)


def gelu_parts(v):
    t = jnp.tanh(GELU_C * (v + GELU_K * v * v * v))
    value = 0.5 * v * (1.0 + t)
    slope = 0.5 * (1.0 + t) + 0.5 * v * (1.0 - t * t) * GELU_C * (1.0 + 3.0 * GELU_K * v * v)
    return value, slope


def gelu_value(v):
    return 0.5 * v * (1.0 + jnp.tanh(GELU_C * (v + GELU_K * v * v * v)))


def row_ids(shape):
    return lax.broadcasted_iota(jnp.int32, shape, 0)


def shift_down(v, k, fill, rows):
    count = v.shape[0]
    if k % 8 == 0:
        return jnp.concatenate([jnp.full((k, v.shape[1]), fill, F32), v[: count - k]], axis=0)
    return jnp.where(rows < k, fill, pltpu.roll(v, k, 0))


def shift_up(v, k, fill, rows):
    count = v.shape[0]
    if k % 8 == 0:
        return jnp.concatenate([v[k:], jnp.full((k, v.shape[1]), fill, F32)], axis=0)
    return jnp.where(rows >= count - k, fill, pltpu.roll(v, count - k, 0))


def run_scan(decay, value, shift, rows):
    k = 1
    while k < value.shape[0]:
        value = value + decay * shift(value, k, 0.0, rows)
        decay = decay * shift(decay, k, 1.0, rows)
        k *= 2
    return decay, value


def conv_kernel(bx_ref, halo_ref, vec_ref, conv_ref, low_ref, ext_ref):
    tokens = bx_ref.shape[1]
    ext_ref[0:8] = halo_ref[0]
    ext_ref[8:] = bx_ref[0].astype(F32)
    total = vec_ref[4:5] + jnp.zeros((tokens, bx_ref.shape[2]), F32)
    for k in range(4):
        total = total + vec_ref[k : k + 1] * ext_ref[8 - k : 8 - k + tokens]
    conv_ref[0] = total
    low_ref[0] = total.astype(BF16)


def gates_kernel(off_ref, win_ref, conv_ref, wg_ref, vec_ref, s0_ref, s1_ref, h_ref, a_ref, end_ref):
    tokens = win_ref.shape[1]
    rows = row_ids((tokens, HALF))
    for m in range(wg_ref.shape[0]):
        cols = slice(m * HALF, (m + 1) * HALF)
        src = pl.multiple_of(off_ref[m], HALF)
        logits = jnp.dot(
            win_ref[0, :, pl.ds(src, 2 * HALF)], wg_ref[m], preferred_element_type=F32
        )
        s0 = jax.nn.sigmoid(logits[:, :HALF] + vec_ref[0:1, cols])
        s1 = jax.nn.sigmoid(logits[:, HALF:] + vec_ref[1:2, cols])
        log_a = vec_ref[2:3, cols] * s0
        value = jnp.sqrt(-expm1_neg(2.0 * log_a)) * (conv_ref[0, :, cols] * s1)
        decay, state = run_scan(jnp.exp(log_a), value, shift_down, rows)
        s0_ref[0, :, cols] = s0
        s1_ref[0, :, cols] = s1
        h_ref[0, :, cols] = state
        a_ref[0, :, cols] = decay
        end_ref[0, 0:1, cols] = state[tokens - 1 :]
        end_ref[0, 1:2, cols] = decay[tokens - 1 :]


def back_scan_kernel(gm_ref, by_ref, st_ref, s0_ref, vec_ref, gy_ref, c_ref, a_ref, end_ref):
    tokens = gm_ref.shape[1]
    rows = row_ids((tokens, HALF))
    for m in range(gm_ref.shape[2] // HALF):
        cols = slice(m * HALF, (m + 1) * HALF)
        gm = gm_ref[0, :, cols]
        value, slope = gelu_parts(by_ref[0, :, cols])
        low = st_ref[0, :, cols].astype(BF16).astype(F32)
        gy_ref[0, :, cols] = (gm * low * slope).astype(BF16)
        grad = (gm * value).astype(BF16).astype(F32)
        decay = jnp.exp(vec_ref[2:3, cols] * s0_ref[0, :, cols])
        prod, carried = run_scan(shift_up(decay, 1, 1.0, rows), grad, shift_up, rows)
        c_ref[0, :, cols] = carried
        a_ref[0, :, cols] = prod
        end_ref[0, 0:1, cols] = decay[0:1] * carried[0:1]
        end_ref[0, 1:2, cols] = decay[0:1] * prod[0:1]


def back_gates_kernel(
    off_ref,
    c_ref,
    a_ref,
    edge_ref,
    s0_ref,
    s1_ref,
    conv_ref,
    st_ref,
    win_ref,
    wg_ref,
    vec_ref,
    gc_ref,
    dw_ref,
    sum_ref,
):
    tokens = c_ref.shape[1]
    rows = row_ids((tokens, HALF))

    @pl.when(pl.program_id(0) == 0)
    def _():
        dw_ref[...] = jnp.zeros_like(dw_ref)
        sum_ref[...] = jnp.zeros_like(sum_ref)

    gc_ref[...] = jnp.zeros_like(gc_ref)
    for m in range(wg_ref.shape[0]):
        cols = slice(m * HALF, (m + 1) * HALF)
        src = pl.multiple_of(off_ref[m], HALF)
        own = pl.multiple_of(off_ref[wg_ref.shape[0]] + m * HALF, HALF)
        carried = c_ref[0, :, cols] + a_ref[0, :, cols] * edge_ref[0, 1:2, cols]
        before = shift_down(st_ref[0, :, cols], 1, 0.0, rows)
        before = jnp.where(rows == 0, edge_ref[0, 0:1, cols], before)
        s0 = s0_ref[0, :, cols]
        s1 = s1_ref[0, :, cols]
        conv = conv_ref[0, :, cols]
        coef = vec_ref[2:3, cols]
        log_a = coef * s0
        root = jnp.sqrt(-expm1_neg(2.0 * log_a))
        g_log = carried * (jnp.exp(log_a) * before - jnp.exp(2.0 * log_a) * (conv * s1) / root)
        g_log = g_log.astype(BF16).astype(F32)
        g_in = (carried * root).astype(BF16).astype(F32)
        rec = (g_log * coef * s0 * (1.0 - s0)).astype(BF16)
        inp = (g_in * conv * s1 * (1.0 - s1)).astype(BF16)
        sum_ref[0:1, cols] += jnp.sum(g_log * s0, axis=0, keepdims=True)
        sum_ref[1:2, cols] += jnp.sum(rec.astype(F32), axis=0, keepdims=True)
        sum_ref[2:3, cols] += jnp.sum(inp.astype(F32), axis=0, keepdims=True)
        both = jnp.concatenate([rec, inp], axis=1)
        gc_ref[0, :, pl.ds(src, 2 * HALF)] += lax.dot_general(
            both, wg_ref[m], (((1,), (1,)), ((), ())), preferred_element_type=F32
        )
        gc_ref[0, :, pl.ds(own, HALF)] += g_in * s1
        dw_ref[m] += lax.dot_general(
            win_ref[0, :, pl.ds(src, 2 * HALF)],
            both,
            (((0,), (0,)), ((), ())),
            preferred_element_type=F32,
        )


def back_conv_kernel(gc_ref, after_ref, bx_ref, halo_ref, vec_ref, gx_ref, sum_ref, g_ext, x_ext):
    tokens = gc_ref.shape[1]

    @pl.when(pl.program_id(0) == 0)
    def _():
        sum_ref[...] = jnp.zeros_like(sum_ref)

    grad = gc_ref[0]
    g_ext[0:tokens] = grad
    g_ext[tokens:] = after_ref[0]
    x_ext[0:8] = halo_ref[0]
    x_ext[8:] = bx_ref[0].astype(F32)
    total = jnp.zeros_like(grad)
    for k in range(4):
        total = total + vec_ref[k : k + 1] * g_ext[k : k + tokens]
        sum_ref[k : k + 1] += jnp.sum(
            grad * x_ext[8 - k : 8 - k + tokens], axis=0, keepdims=True
        )
    sum_ref[4:5] += jnp.sum(grad, axis=0, keepdims=True)
    gx_ref[0] = total.astype(BF16)


def slot_spec(rows, width):
    return pl.BlockSpec((1, rows, width), lambda i: (i, 0, 0))


def whole_spec(shape):
    zero = (0,) * len(shape)
    return pl.BlockSpec(shape, lambda i: zero)


def call(kernel, slots, ins, in_specs, outs, out_specs, scratch=()):
    return pl.pallas_call(
        kernel,
        grid=(slots,),
        in_specs=in_specs,
        out_specs=out_specs,
        out_shape=outs,
        scratch_shapes=list(scratch),
    )(*ins)


def rms_scale(values):
    return lax.rsqrt(jnp.mean(values * values, axis=-1, keepdims=True) + EPS)


def dot_nt(a, b):
    return lax.dot_general(a, b, (((1,), (1,)), ((), ())), preferred_element_type=F32)


def dot_nn(a, b):
    return jnp.dot(a, b, preferred_element_type=F32)


def on_device(
    block_in,
    cotangent,
    w_x,
    w_y,
    w_out,
    w_gate,
    w_up,
    w_down,
    norm1_gain,
    norm2_gain,
    conv_weight,
    conv_bias,
    gate_weight,
    gate_bias,
    decay_param,
):
    slots = lax.axis_size("wshard")
    place = lax.axis_index("wshard")
    count = lax.axis_size("seq")
    spot = lax.axis_index("seq")
    x_own = block_in[0]
    g_own = cotangent[0]
    tokens, model = x_own.shape
    chans = w_x.shape[0]
    heads, inner = gate_weight.shape[1], gate_weight.shape[3]
    taps = conv_weight.shape[0]
    blocks = chans // HALF
    offset = (chans * place) % inner
    window = -(-(chans + (chans % inner)) // inner) * inner
    odd = offset != 0
    bits = bits_of(count)
    order_a = bits
    order_b = bits[:1] + bits[1:][::-1]
    slot_rows = slots * tokens

    def by_slot(v):
        return v.reshape(slots, tokens, v.shape[-1])

    def flat(v):
        return v.reshape(slot_rows, v.shape[-1])

    def split(v):
        return [v[k * tokens : (k + 1) * tokens] for k in range(slots)]

    gains = all_parts(jnp.stack([norm1_gain, norm2_gain]))
    gains = jnp.swapaxes(gains, 0, 1).reshape(2, model).astype(F32)
    gain_one, gain_two = gains[0:1], gains[1:2]
    conv_vec = jnp.concatenate(
        [conv_weight.astype(F32), conv_bias.astype(F32)[None], jnp.zeros((3, chans), F32)], axis=0
    )
    decay = decay_param.astype(F32)
    coef = -DECAY_SCALE * jax.nn.softplus(-decay)
    gate_vec = jnp.concatenate(
        [gate_bias.astype(F32), coef[None], jnp.zeros((5, chans), F32)], axis=0
    )
    offs = jnp.concatenate(
        [
            (offset + HALF * jnp.arange(blocks, dtype=jnp.int32)) // inner * inner,
            offset[None].astype(jnp.int32),
        ]
    ).astype(jnp.int32)

    x_all = jnp.concatenate(relay_gather(x_own), axis=0)
    g_all = jnp.concatenate(relay_gather(g_own), axis=0)
    x_f = x_all.astype(F32)
    x_hat = x_f * rms_scale(x_f)
    normed_one = (x_hat * gain_one).astype(BF16)

    gate_cols = jnp.transpose(gate_weight, (0, 2, 1, 3)).reshape(2, -1, slots, chans)
    gate_cols = swap_parts(jnp.moveaxis(gate_cols, 2, 0))
    gate_cols = jnp.moveaxis(gate_cols, 0, 1).reshape(2, inner, blocks, HALF)
    wg = jnp.transpose(gate_cols, (2, 1, 0, 3)).reshape(blocks, inner, 2 * HALF)

    branch_x = by_slot(dot_nt(normed_one, w_x).astype(BF16))
    halo = lax.ppermute(
        branch_x[:, tokens - 8 :], "seq", [(i, i + 1) for i in range(count - 1)]
    ).astype(F32)
    branch_y = by_slot(dot_nt(normed_one, w_y))
    conv, conv_low = call(
        conv_kernel,
        slots,
        (branch_x, halo, conv_vec),
        [slot_spec(tokens, chans), slot_spec(8, chans), whole_spec((8, chans))],
        (
            jax.ShapeDtypeStruct((slots, tokens, chans), F32),
            jax.ShapeDtypeStruct((slots, tokens, chans), BF16),
        ),
        (slot_spec(tokens, chans), slot_spec(tokens, chans)),
        [pltpu.VMEM((tokens + 8, chans), F32)],
    )
    extra = window - chans

    def partner(first, last):
        moved = jnp.where(odd, jnp.roll(first, -1, axis=0), jnp.roll(last, 1, axis=0))
        return exchange_pair(moved, "wshard", 1)

    lent = partner(conv_low[:, :, :extra], conv_low[:, :, chans - extra :])
    win = jnp.where(
        odd,
        jnp.concatenate([lent, conv_low], axis=2),
        jnp.concatenate([conv_low, lent], axis=2),
    )
    smem = pl.BlockSpec(memory_space=pltpu.SMEM)
    wide = jax.ShapeDtypeStruct((slots, tokens, chans), F32)
    edge = jax.ShapeDtypeStruct((slots, 8, chans), F32)
    s_rec, s_in, h_local, a_prod, ends = call(
        gates_kernel,
        slots,
        (offs, win, conv, wg, gate_vec),
        [
            smem,
            slot_spec(tokens, window),
            slot_spec(tokens, chans),
            whole_spec(wg.shape),
            whole_spec((8, chans)),
        ],
        (wide, wide, wide, wide, edge),
        (slot_spec(tokens, chans),) * 4 + (slot_spec(8, chans),),
    )
    ends = lax.all_gather(ends[:, :2], "seq", axis=0)
    carry = jnp.zeros((slots, chans), F32)
    for r in range(count - 1):
        carry = jnp.where(r < spot, ends[r, :, 0] + ends[r, :, 1] * carry, carry)
    state = h_local + a_prod * carry[:, None, :]
    gelu_y = gelu_value(branch_y)
    mixed = flat((gelu_y * state.astype(BF16).astype(F32)).astype(BF16))

    residual = x_own.astype(F32) + relay_scatter(split(dot_nn(mixed, w_out)))
    res_scale = rms_scale(residual)
    res_hat = residual * res_scale
    normed_two = jnp.concatenate(relay_gather((res_hat * gain_two).astype(BF16)), axis=0)

    gate = dot_nt(normed_two, w_gate)
    up = dot_nt(normed_two, w_up)
    grad_activ = dot_nt(g_all, w_down)
    gelu_g, slope_g = gelu_parts(gate)
    activ = (gelu_g * up).astype(BF16)
    grad_gate = (grad_activ * up * slope_g).astype(BF16)
    grad_up = (grad_activ * gelu_g).astype(BF16)
    grad_two = relay_scatter(split(dot_nn(grad_gate, w_gate) + dot_nn(grad_up, w_up)))
    block_out = (residual + relay_scatter(split(dot_nn(activ, w_down)))).astype(BF16)

    scaled = grad_two * gain_two
    grad_residual = g_own.astype(F32) + res_scale * (
        scaled - res_hat * jnp.mean(scaled * res_hat, axis=-1, keepdims=True)
    )
    grad_norm2 = jnp.sum(grad_two * res_hat, axis=0)
    grad_proj = jnp.concatenate(relay_gather(grad_residual.astype(BF16)), axis=0)

    g_cols = xor_columns(g_all, order_a)
    two_a = xor_columns(normed_two, order_a)
    two_b = xor_columns(normed_two, order_b)
    grad_w_down = halving_grad(activ, g_cols, order_a)
    grad_w_gate = halving_grad(grad_gate, two_b, order_b)
    grad_w_up = halving_grad(grad_up, two_a, order_a)

    grad_mixed = by_slot(dot_nt(grad_proj, w_out))
    grad_y, c_local, c_prod, back_ends = call(
        back_scan_kernel,
        slots,
        (grad_mixed, branch_y, state, s_rec, gate_vec),
        [slot_spec(tokens, chans)] * 4 + [whole_spec((8, chans))],
        (jax.ShapeDtypeStruct((slots, tokens, chans), BF16), wide, wide, edge),
        (slot_spec(tokens, chans),) * 3 + (slot_spec(8, chans),),
    )
    back_ends = lax.all_gather(back_ends[:, :2], "seq", axis=0)
    back = jnp.zeros((slots, chans), F32)
    for r in range(count - 1, 0, -1):
        back = jnp.where(r > spot, back_ends[r, :, 0] + back_ends[r, :, 1] * back, back)
    edges = jnp.concatenate(
        [carry[:, None], back[:, None], jnp.zeros((slots, 6, chans), F32)], axis=1
    )
    grad_win, grad_wg, gate_sums = call(
        back_gates_kernel,
        slots,
        (offs, c_local, c_prod, edges, s_rec, s_in, conv, state, win, wg, gate_vec),
        [smem]
        + [slot_spec(tokens, chans)] * 2
        + [slot_spec(8, chans)]
        + [slot_spec(tokens, chans)] * 4
        + [slot_spec(tokens, window), whole_spec(wg.shape), whole_spec((8, chans))],
        (
            jax.ShapeDtypeStruct((slots, tokens, window), F32),
            jax.ShapeDtypeStruct(wg.shape, F32),
            jax.ShapeDtypeStruct((8, chans), F32),
        ),
        (slot_spec(tokens, window), whole_spec(wg.shape), whole_spec((8, chans))),
    )
    near = jnp.where(odd, grad_win[:, :, extra:], grad_win[:, :, :chans])
    got = partner(grad_win[:, :, :extra], grad_win[:, :, chans:])
    blank = jnp.zeros((slots, tokens, chans - extra), F32)
    grad_conv = near + jnp.where(
        odd, jnp.concatenate([got, blank], axis=2), jnp.concatenate([blank, got], axis=2)
    )
    after = lax.ppermute(grad_conv[:, :8], "seq", [(i + 1, i) for i in range(count - 1)])
    grad_x_low, conv_sums = call(
        back_conv_kernel,
        slots,
        (grad_conv, after, branch_x, halo, conv_vec),
        [
            slot_spec(tokens, chans),
            slot_spec(8, chans),
            slot_spec(tokens, chans),
            slot_spec(8, chans),
            whole_spec((8, chans)),
        ],
        (
            jax.ShapeDtypeStruct((slots, tokens, chans), BF16),
            jax.ShapeDtypeStruct((8, chans), F32),
        ),
        (slot_spec(tokens, chans), whole_spec((8, chans))),
        [pltpu.VMEM((tokens + 8, chans), F32), pltpu.VMEM((tokens + 8, chans), F32)],
    )
    grad_x_low = flat(grad_x_low)
    grad_y = flat(grad_y)
    one_part = dot_nn(grad_x_low, w_x) + dot_nn(grad_y, w_y)
    grad_norm1 = jnp.sum(one_part * x_hat, axis=0)
    grad_one = relay_scatter(split(one_part))
    own_f = x_own.astype(F32)
    own_scale = rms_scale(own_f)
    own_hat = own_f * own_scale
    scaled_one = grad_one * gain_one
    grad_input = grad_residual + own_scale * (
        scaled_one - own_hat * jnp.mean(scaled_one * own_hat, axis=-1, keepdims=True)
    )

    proj_cols = xor_columns(grad_proj, order_b)
    one_a = xor_columns(normed_one, order_a)
    one_b = xor_columns(normed_one, order_b)
    grad_w_out = halving_grad(mixed, proj_cols, order_b)
    grad_w_x = halving_grad(grad_x_low, one_a, order_a)
    grad_w_y = halving_grad(grad_y, one_b, order_b)

    norms = sum_all(jnp.stack([grad_norm1, grad_norm2]), "wshard")
    norms = lax.dynamic_slice_in_dim(norms, place * chans, chans, 1)
    smalls = sum_all(jnp.concatenate([norms, gate_sums[:3], conv_sums[:5]], axis=0), "seq")
    gate_parts = grad_wg.reshape(blocks, inner, 2, HALF)
    gate_parts = jnp.transpose(gate_parts, (1, 2, 0, 3)).reshape(slots, -1, 2, chans)
    gate_parts = sum_all(swap_parts(gate_parts), "seq")
    gate_parts = jnp.transpose(gate_parts, (2, 1, 0, 3)).reshape(2, -1, heads, inner)
    grad_gates = jnp.transpose(gate_parts, (0, 2, 1, 3))

    return (
        block_out[None],
        grad_input[None],
        grad_w_x,
        grad_w_y,
        grad_w_out,
        grad_w_gate,
        grad_w_up,
        grad_w_down,
        smalls[0],
        smalls[1],
        smalls[5:9],
        smalls[9],
        grad_gates,
        smalls[3:5],
        DECAY_SCALE * jax.nn.sigmoid(-decay) * smalls[2],
    )


def solution(mesh):
    row = P("wshard", None)
    vec = P("wshard")
    tok = P("wshard", "seq", None)
    grad = P("wshard", "seq")
    return jax.shard_map(
        on_device,
        mesh=mesh,
        in_specs=(
            tok,
            tok,
            row,
            row,
            row,
            row,
            row,
            row,
            vec,
            vec,
            P(None, "wshard"),
            vec,
            P(None, None, "wshard", None),
            P(None, "wshard"),
            vec,
        ),
        out_specs=(
            tok,
            tok,
            grad,
            grad,
            grad,
            grad,
            grad,
            grad,
            vec,
            vec,
            P(None, "wshard"),
            vec,
            P(None, None, "wshard", None),
            P(None, "wshard"),
            vec,
        ),
        check_vma=False,
    )
```

```python
import functools

import jax
import jax.numpy as jnp
from jax import lax
from jax.experimental import pallas as pl
from jax.experimental.pallas import tpu as pltpu
from jax.sharding import PartitionSpec as P

EPS = 1e-06
DECAY_SCALE = 8.0
HALF = 128
GELU_C = 0.7978845608028654
GELU_K = 0.044715
F32 = jnp.float32
BF16 = jnp.bfloat16
OWN, FAR, LEND, SLOT, REL = 16, 17, 18, 19, 20


def ring(value, axis="wshard"):
    count = lax.axis_size(axis)
    return lax.ppermute(value, axis, [(i, (i + 1) % count) for i in range(count)])


def ring_gather(part, axis="wshard"):
    slots = [part]
    for _ in range(1, lax.axis_size(axis)):
        slots.append(ring(slots[-1], axis))
    return slots


def join(*values):
    return lax.optimization_barrier(values)


def ring_add(slot, total, axis="wshard"):
    mine = slot if total is None else slot.astype(F32) + total.astype(F32)
    mine = mine.astype(BF16)
    return mine, ring(mine, axis)


def ring_scatter(slots, axis="wshard"):
    total = None
    for slot in slots[1:]:
        _, total = ring_add(slot, total, axis)
    return slots[0] + total.astype(F32)


def tie(value, *others):
    return lax.optimization_barrier((value,) + others)[0]


def exchange_pair(value, axis, bit):
    count = lax.axis_size(axis)
    return lax.ppermute(value, axis, [(i, i ^ bit) for i in range(count)])


def bits_of(count):
    return [1 << i for i in range(count.bit_length() - 1)]


def sum_all(value, axis):
    for bit in bits_of(lax.axis_size(axis)):
        value = value + exchange_pair(value, axis, bit)
    return value


def from_slots(slots, axis="wshard"):
    count = lax.axis_size(axis)
    place = lax.axis_index(axis)
    back = jnp.stack(slots[::-1] + slots[::-1])
    return lax.dynamic_slice_in_dim(back, count - 1 - place, count, 0)


def all_parts(part, axis="wshard"):
    count = lax.axis_size(axis)
    slots = [part] + [
        lax.ppermute(part, axis, [(i, (i + k) % count) for i in range(count)])
        for k in range(1, count)
    ]
    return from_slots(slots, axis)


def swap_parts(parts, axis="wshard"):
    count = lax.axis_size(axis)
    place = lax.axis_index(axis)
    slots = []
    for k in range(count):
        mine = lax.dynamic_index_in_dim(parts, (place + k) % count, 0, keepdims=False)
        if k:
            mine = lax.ppermute(mine, axis, [(i, (i + k) % count) for i in range(count)])
        slots.append(mine)
    return from_slots(slots, axis)


def relative_order(count, order):
    offsets = [0]
    for bit in reversed(order):
        offsets = offsets + [o | bit for o in offsets]
    return offsets


def prefix_step(state, bit, back, axis="seq"):
    total, before = state
    other = exchange_pair(total, axis, bit)
    high = (lax.axis_index(axis) & bit) != 0
    first = high != back
    before = jnp.stack(
        [
            jnp.where(first, before[:, 0] + before[:, 1] * other[:, 0], before[:, 0]),
            jnp.where(first, before[:, 1] * other[:, 1], before[:, 1]),
        ],
        axis=1,
    )
    total = jnp.stack(
        [
            jnp.where(
                first,
                total[:, 0] + total[:, 1] * other[:, 0],
                other[:, 0] + other[:, 1] * total[:, 0],
            ),
            total[:, 1] * other[:, 1],
        ],
        axis=1,
    )
    return total, before


def prefix_start(ends):
    ones = jnp.ones_like(ends[:, 0])
    return ends, jnp.stack([jnp.zeros_like(ones), ones], axis=1)


def rank_of(offset, order):
    rank = jnp.int32(0)
    for i, bit in enumerate(order):
        rank = rank + jnp.where((offset & bit) != 0, 1 << (len(order) - 1 - i), 0)
    return rank


def turn_kernel(at_ref, *refs, slots):
    outs, held_ref = refs[slots:-1], refs[-1]
    row = 0
    for ref in refs[:slots]:
        for col in range(0, ref.shape[1], HALF):
            held_ref[col : col + HALF, row : row + ref.shape[0]] = ref[:, col : col + HALF].T
        row += ref.shape[0]
    count = at_ref.shape[1]
    width = held_ref.shape[0] // count
    for out, ref in enumerate(outs):
        for q in range(count):
            start = pl.multiple_of(at_ref[out, q], 16)
            ref[q * width : (q + 1) * width] = held_ref[pl.ds(start, width)]


def turned(parts, orders, axis="seq"):
    count = lax.axis_size(axis)
    place = lax.axis_index(axis)
    model = parts[0].shape[1]
    rows = sum(part.shape[0] for part in parts)
    width = model // count
    at = [(place ^ jnp.array(relative_order(count, order), jnp.int32)) * width for order in orders]
    vmem = pl.BlockSpec(memory_space=pltpu.VMEM)
    return pl.pallas_call(
        functools.partial(turn_kernel, slots=len(parts)),
        in_specs=[pl.BlockSpec(memory_space=pltpu.SMEM)] + [vmem] * len(parts),
        out_specs=(vmem,) * len(orders),
        out_shape=(jax.ShapeDtypeStruct((model, rows), parts[0].dtype),) * len(orders),
        scratch_shapes=[pltpu.VMEM((model, rows), parts[0].dtype)],
    )(jnp.stack(at).astype(jnp.int32), *parts)


class Halving:
    def __init__(self, left, right, order, extra=None, axis="seq"):
        self.left, self.right, self.order, self.axis = left, right, list(order), axis
        self.extra = extra
        self.held = []
        self.size = left.shape[0]

    def part(self, lo, hi, after):
        width = self.right.shape[1]
        right = tie(self.right, *after) if after else self.right
        total = dot_nn(self.left[lo:hi], right)
        for piece in self.held:
            total = total + piece[lo:hi, :width].astype(F32)
        if self.extra is None:
            return total, None
        more = self.extra[lo:hi]
        for piece in self.held:
            more = more + piece[lo:hi, width:].astype(F32)
        return total, more

    def give(self, *after):
        total, more = self.part(self.size // 2, self.size, after)
        total = total.astype(BF16)
        return total if more is None else jnp.concatenate([total, more.astype(BF16)], axis=1)

    def send(self, half):
        self.held.append(exchange_pair(half, self.axis, self.order.pop(0)))
        self.size //= 2

    def finish(self, *after):
        while self.order:
            self.send(self.give(*after))
        total, more = self.part(0, self.size, after)
        return (total.T,) if more is None else (total.T, more)


def norm_kernel(x_ref, part_ref, out_ref):
    @pl.when(pl.program_id(0) == 0)
    def _():
        out_ref[...] = jnp.zeros_like(out_ref)

    values = x_ref[...].astype(F32)
    out_ref[...] += jnp.sum(part_ref[...] * (values * rms_scale(values)), axis=0, keepdims=True)


def norm_grad(x, part, slots):
    spec = pl.BlockSpec((x.shape[0] // slots, x.shape[1]), lambda i: (i, 0))
    return pl.pallas_call(
        norm_kernel,
        grid=(slots,),
        in_specs=[spec, spec],
        out_specs=pl.BlockSpec((1, x.shape[1]), lambda i: (0, 0)),
        out_shape=jax.ShapeDtypeStruct((1, x.shape[1]), F32),
    )(x, part)


def expm1_neg(v):
    poly = 1.0 + v / 9.0
    for n in range(8, 1, -1):
        poly = 1.0 + poly * v / float(n)
    return jnp.where(v > -0.5, v * poly, jnp.exp(v) - 1.0)


def gelu_parts(v):
    t = jnp.tanh(GELU_C * (v + GELU_K * v * v * v))
    value = 0.5 * v * (1.0 + t)
    slope = 0.5 * (1.0 + t) + 0.5 * v * (1.0 - t * t) * GELU_C * (1.0 + 3.0 * GELU_K * v * v)
    return value, slope


def gelu_value(v):
    return 0.5 * v * (1.0 + jnp.tanh(GELU_C * (v + GELU_K * v * v * v)))


def row_ids(shape):
    return lax.broadcasted_iota(jnp.int32, shape, 0)


def shift_down(v, k, fill, rows):
    count = v.shape[0]
    if k % 8 == 0:
        return jnp.concatenate([jnp.full((k, v.shape[1]), fill, F32), v[: count - k]], axis=0)
    return jnp.where(rows < k, fill, pltpu.roll(v, k, 0))


def shift_up(v, k, fill, rows):
    count = v.shape[0]
    if k % 8 == 0:
        return jnp.concatenate([v[k:], jnp.full((k, v.shape[1]), fill, F32)], axis=0)
    return jnp.where(rows >= count - k, fill, pltpu.roll(v, count - k, 0))


def run_scan(decay, value, shift, rows):
    k = 1
    while k < value.shape[0]:
        value = value + decay * shift(value, k, 0.0, rows)
        decay = decay * shift(decay, k, 1.0, rows)
        k *= 2
    return decay, value


def assemble_kernel(at_ref, *refs):
    out_ref = refs[-1]
    for i, ref in enumerate(refs[:-1]):
        for j in range(ref.shape[0]):
            row = pl.multiple_of(at_ref[i, j], 16)
            for m in range(out_ref.shape[0]):
                for g in range(2):
                    out_ref[m, pl.ds(row, 16), g * HALF : (g + 1) * HALF] = ref[
                        j, g, :, m * HALF : (m + 1) * HALF
                    ]


def branch_kernel(x_ref, gain_ref, wx_ref, wy_ref, *refs):
    n_ref, bx_ref, by_ref = refs[-3:]
    values = x_ref[...].astype(F32)
    low = (values * rms_scale(values) * gain_ref[...]).astype(BF16)
    n_ref[...] = low
    bx_ref[0] = dot_nt(low, wx_ref[...]).astype(BF16)
    by_ref[0] = dot_nt(low, wy_ref[...])


def branch_call(x, gain, w_x, w_y, held, slots, place):
    rows, model = x.shape
    chans = w_x.shape[0]
    kept = pl.BlockSpec(memory_space=pl.ANY)
    whole = lambda shape: pl.BlockSpec(shape, lambda i: (0,) * len(shape))
    out = pl.BlockSpec((1, rows, chans), lambda i: (place, 0, 0))
    return pl.pallas_call(
        branch_kernel,
        grid=(1,),
        in_specs=[whole(x.shape), whole(gain.shape), whole(w_x.shape), whole(w_y.shape)]
        + [kept] * len(held),
        out_specs=(pl.BlockSpec((rows, model), lambda i: (place, 0)), out, out),
        out_shape=(
            jax.ShapeDtypeStruct((slots * rows, model), BF16),
            jax.ShapeDtypeStruct((slots, rows, chans), BF16),
            jax.ShapeDtypeStruct((slots, rows, chans), F32),
        ),
        input_output_aliases={4 + i: i for i in range(len(held))},
    )(x, gain, w_x, w_y, *held)


def conv_kernel(off_ref, bx_ref, halo_ref, vec_ref, conv_ref, low_ref, lend_ref, ext_ref):
    tokens = bx_ref.shape[1]
    ext_ref[0:8] = halo_ref[0]
    ext_ref[8:] = bx_ref[0].astype(F32)
    total = vec_ref[4:5] + jnp.zeros((tokens, bx_ref.shape[2]), F32)
    for k in range(4):
        total = total + vec_ref[k : k + 1] * ext_ref[8 - k : 8 - k + tokens]
    conv_ref[0] = total
    low_ref[0] = total.astype(BF16)
    lend_ref[0] = low_ref[0, :, pl.ds(pl.multiple_of(off_ref[LEND], HALF), lend_ref.shape[2])]


def gates_kernel(
    off_ref, low_ref, lent_ref, conv_ref, wg_ref, vec_ref,
    s0_ref, s1_ref, h_ref, a_ref, end_ref, win_ref,
):
    tokens = win_ref.shape[1]
    rows = row_ids((tokens, HALF))
    own = pl.multiple_of(off_ref[OWN], HALF)
    far = pl.multiple_of(off_ref[FAR], HALF)
    win_ref[0, :, pl.ds(own, low_ref.shape[2])] = low_ref[0]
    win_ref[0, :, pl.ds(far, lent_ref.shape[2])] = lent_ref[0]
    for m in range(wg_ref.shape[0]):
        cols = slice(m * HALF, (m + 1) * HALF)
        src = pl.multiple_of(off_ref[m], HALF)
        logits = jnp.dot(
            win_ref[0, :, pl.ds(src, 2 * HALF)], wg_ref[m], preferred_element_type=F32
        )
        s0 = jax.nn.sigmoid(logits[:, :HALF] + vec_ref[0:1, cols])
        s1 = jax.nn.sigmoid(logits[:, HALF:] + vec_ref[1:2, cols])
        log_a = vec_ref[2:3, cols] * s0
        value = jnp.sqrt(-expm1_neg(2.0 * log_a)) * (conv_ref[0, :, cols] * s1)
        decay, state = run_scan(jnp.exp(log_a), value, shift_down, rows)
        s0_ref[0, :, cols] = s0
        s1_ref[0, :, cols] = s1
        h_ref[0, :, cols] = state
        a_ref[0, :, cols] = decay
        end_ref[0, 0:1, cols] = state[tokens - 1 :]
        end_ref[0, 1:2, cols] = decay[tokens - 1 :]


def back_scan_kernel(
    off_ref, gm_ref, by_ref, st_ref, s0_ref, vec_ref, gy_ref, c_ref, a_ref, end_ref
):
    tokens = gm_ref.shape[1]
    rows = row_ids((tokens, HALF))
    for m in range(gm_ref.shape[2] // HALF):
        cols = slice(m * HALF, (m + 1) * HALF)
        gm = gm_ref[0, :, cols]
        value, slope = gelu_parts(by_ref[0, :, cols])
        low = st_ref[0, :, cols].astype(BF16).astype(F32)
        gy_ref[0, :, cols] = (gm * low * slope).astype(BF16)
        grad = (gm * value).astype(BF16).astype(F32)
        decay = jnp.exp(vec_ref[2:3, cols] * s0_ref[0, :, cols])
        prod, carried = run_scan(shift_up(decay, 1, 1.0, rows), grad, shift_up, rows)
        c_ref[0, :, cols] = carried
        a_ref[0, :, cols] = prod
        end_ref[0, 0:1, cols] = decay[0:1] * carried[0:1]
        end_ref[0, 1:2, cols] = decay[0:1] * prod[0:1]


def back_gates_kernel(
    off_ref,
    c_ref,
    a_ref,
    edge_ref,
    s0_ref,
    s1_ref,
    conv_ref,
    st_ref,
    win_ref,
    wg_ref,
    vec_ref,
    near_ref,
    far_ref,
    piece_ref,
    sum_ref,
    dw_ref,
    gc_ref,
    *,
    count,
    planes,
):
    tokens = c_ref.shape[1]
    rows = row_ids((tokens, HALF))

    @pl.when(pl.program_id(0) == 0)
    def _():
        dw_ref[...] = jnp.zeros_like(dw_ref)
        sum_ref[...] = jnp.zeros_like(sum_ref)

    gc_ref[...] = jnp.zeros_like(gc_ref)
    for m in range(wg_ref.shape[0]):
        cols = slice(m * HALF, (m + 1) * HALF)
        src = pl.multiple_of(off_ref[m], HALF)
        own = pl.multiple_of(off_ref[OWN] + m * HALF, HALF)
        carried = c_ref[0, :, cols] + a_ref[0, :, cols] * edge_ref[0, 1:2, cols]
        before = shift_down(st_ref[0, :, cols], 1, 0.0, rows)
        before = jnp.where(rows == 0, edge_ref[0, 0:1, cols], before)
        s0 = s0_ref[0, :, cols]
        s1 = s1_ref[0, :, cols]
        conv = conv_ref[0, :, cols]
        coef = vec_ref[2:3, cols]
        log_a = coef * s0
        root = jnp.sqrt(-expm1_neg(2.0 * log_a))
        g_log = carried * (jnp.exp(log_a) * before - jnp.exp(2.0 * log_a) * (conv * s1) / root)
        g_log = g_log.astype(BF16).astype(F32)
        g_in = (carried * root).astype(BF16).astype(F32)
        rec = (g_log * coef * s0 * (1.0 - s0)).astype(BF16)
        inp = (g_in * conv * s1 * (1.0 - s1)).astype(BF16)
        sum_ref[0:1, cols] += jnp.sum(g_log * s0, axis=0, keepdims=True)
        sum_ref[1:2, cols] += jnp.sum(rec.astype(F32), axis=0, keepdims=True)
        sum_ref[2:3, cols] += jnp.sum(inp.astype(F32), axis=0, keepdims=True)
        both = jnp.concatenate([rec, inp], axis=1)
        gc_ref[:, pl.ds(src, 2 * HALF)] += lax.dot_general(
            both, wg_ref[m], (((1,), (1,)), ((), ())), preferred_element_type=F32
        )
        gc_ref[:, pl.ds(own, HALF)] += g_in * s1
        dw_ref[m] += lax.dot_general(
            win_ref[0, :, pl.ds(src, 2 * HALF)],
            both,
            (((0,), (0,)), ((), ())),
            preferred_element_type=F32,
        )

    own = pl.multiple_of(off_ref[OWN], HALF)
    far = pl.multiple_of(off_ref[FAR], HALF)
    near_ref[0] = gc_ref[:, pl.ds(own, near_ref.shape[2])]
    far_ref[0] = gc_ref[:, pl.ds(far, far_ref.shape[2])]

    @pl.when(pl.program_id(0) == pl.num_programs(0) - 1)
    def _():
        blocks = dw_ref.shape[0]
        width = dw_ref.shape[1] // (planes * count)
        if width % 8:
            piece_ref[...] = dw_ref[...]
            return
        row = 0
        for q in range(count):
            for j in range(planes):
                first = pl.multiple_of((j * count + off_ref[REL + q]) * width, width)
                for g in range(2):
                    for m in range(blocks):
                        piece_ref[row : row + width] = dw_ref[
                            m, pl.ds(first, width), g * HALF : (g + 1) * HALF
                        ]
                        row += width


def back_conv_kernel(
    off_ref, gc_ref, got_ref, after_ref, bx_ref, halo_ref, vec_ref, gx_ref, sum_ref, g_ext, x_ext
):
    tokens = gc_ref.shape[1]

    @pl.when(pl.program_id(0) == 0)
    def _():
        sum_ref[...] = jnp.zeros_like(sum_ref)

    lend = pl.multiple_of(off_ref[LEND], HALF)
    g_ext[0:tokens] = gc_ref[0]
    g_ext[0:tokens, pl.ds(lend, got_ref.shape[2])] += got_ref[0]
    grad = g_ext[0:tokens]
    g_ext[tokens:] = after_ref[0]
    x_ext[0:8] = halo_ref[0]
    x_ext[8:] = bx_ref[0].astype(F32)
    total = jnp.zeros_like(grad)
    for k in range(4):
        total = total + vec_ref[k : k + 1] * g_ext[k : k + tokens]
        sum_ref[k : k + 1] += jnp.sum(
            grad * x_ext[8 - k : 8 - k + tokens], axis=0, keepdims=True
        )
    sum_ref[4:5] += jnp.sum(grad, axis=0, keepdims=True)
    gx_ref[0] = total.astype(BF16)


def ffn_kernel(two_ref, g_ref, wg_ref, wu_ref, wd_ref, *refs):
    act_ref, gate_ref, up_ref, part_ref, total_ref = refs[-5:]
    step = pl.program_id(0)
    gate = dot_nt(two_ref[...], wg_ref[...])
    up = dot_nt(two_ref[...], wu_ref[...])
    grad = dot_nt(g_ref[...], wd_ref[...])
    value, slope = gelu_parts(gate)
    act_ref[...] = (value * up).astype(BF16)
    grad_gate = (grad * up * slope).astype(BF16)
    grad_up = (grad * value).astype(BF16)
    gate_ref[...] = grad_gate
    up_ref[...] = grad_up
    part = dot_nn(grad_gate, wg_ref[...]) + dot_nn(grad_up, wu_ref[...])

    @pl.when(step == 0)
    def _():
        total_ref[...] = part

    @pl.when(step > 0)
    def _():
        total_ref[...] += part

    @pl.when(step == pl.num_programs(0) - 1)
    def _():
        part_ref[...] = total_ref[...].astype(part_ref.dtype)


def ffn_call(two, grad, w_gate, w_up, w_down, held, slots, place, kind):
    rows, model = two.shape
    hidden = w_gate.shape[0]
    width = next(w for w in (384, 256, HALF) if hidden % w == 0)
    tok = pl.BlockSpec((rows, model), lambda i: (0, 0))
    weight = pl.BlockSpec((width, model), lambda i: (i, 0))
    wide = pl.BlockSpec((rows, width), lambda i: (place, i))
    kept = pl.BlockSpec(memory_space=pl.ANY)
    return pl.pallas_call(
        ffn_kernel,
        grid=(hidden // width,),
        in_specs=[tok, tok, weight, weight, weight] + [kept] * len(held),
        out_specs=(wide,) * 3 + (tok,),
        out_shape=(jax.ShapeDtypeStruct((slots * rows, hidden), BF16),) * 3
        + (jax.ShapeDtypeStruct((rows, model), kind),),
        scratch_shapes=[pltpu.VMEM((rows, model), F32)],
        input_output_aliases={5 + i: i for i in range(len(held))},
    )(two, grad, w_gate, w_up, w_down, *held)


def slot_spec(rows, width):
    return pl.BlockSpec((1, rows, width), lambda i, off: (i, 0, 0))


def partner_spec(rows, width, slots):
    return pl.BlockSpec((1, rows, width), lambda i, off: ((i + off[SLOT]) % slots, 0, 0))


def whole_spec(shape):
    zero = (0,) * len(shape)
    return pl.BlockSpec(shape, lambda i, off: zero)


def call(kernel, slots, offs, ins, in_specs, outs, out_specs, scratch=()):
    return pl.pallas_call(
        kernel,
        grid_spec=pltpu.PrefetchScalarGridSpec(
            num_scalar_prefetch=1,
            grid=(slots,),
            in_specs=in_specs,
            out_specs=out_specs,
            scratch_shapes=list(scratch),
        ),
        out_shape=outs,
    )(offs, *ins)


def rms_scale(values):
    return lax.rsqrt(jnp.mean(values * values, axis=-1, keepdims=True) + EPS)


def dot_nt(a, b):
    return lax.dot_general(a, b, (((1,), (1,)), ((), ())), preferred_element_type=F32)


def dot_nn(a, b):
    return jnp.dot(a, b, preferred_element_type=F32)


def on_device(
    block_in,
    cotangent,
    w_x,
    w_y,
    w_out,
    w_gate,
    w_up,
    w_down,
    norm1_gain,
    norm2_gain,
    conv_weight,
    conv_bias,
    gate_weight,
    gate_bias,
    decay_param,
):
    slots = lax.axis_size("wshard")
    place = lax.axis_index("wshard")
    count = lax.axis_size("seq")
    spot = lax.axis_index("seq")
    x_own = block_in[0]
    g_own = cotangent[0]
    tokens, model = x_own.shape
    chans = w_x.shape[0]
    heads, inner = gate_weight.shape[1], gate_weight.shape[3]
    taps = conv_weight.shape[0]
    blocks = chans // HALF
    offset = (chans * place) % inner
    window = -(-(chans + (chans % inner)) // inner) * inner
    odd = offset != 0
    bits = bits_of(count)
    order_a = bits
    order_b = bits[:1] + bits[1:][::-1]
    slot_rows = slots * tokens

    def by_slot(v):
        return v.reshape(slots, tokens, v.shape[-1])

    def flat(v):
        return v.reshape(slot_rows, v.shape[-1])

    def split(v):
        return [v[k * tokens : (k + 1) * tokens] for k in range(slots)]

    x_slots = [x_own, ring(x_own)]
    gains = all_parts(tie(jnp.stack([norm1_gain, norm2_gain]), x_slots[1]))
    gains = jnp.swapaxes(gains, 0, 1).reshape(2, model).astype(F32)
    gain_one, gain_two = gains[0:1], gains[1:2]
    conv_vec = jnp.concatenate(
        [conv_weight.astype(F32), conv_bias.astype(F32)[None], jnp.zeros((3, chans), F32)], axis=0
    )
    decay = decay_param.astype(F32)
    coef = -DECAY_SCALE * jax.nn.softplus(-decay)
    gate_vec = jnp.concatenate(
        [gate_bias.astype(F32), coef[None], jnp.zeros((5, chans), F32)], axis=0
    )
    extra = window - chans
    offs = jnp.concatenate(
        [
            (offset + HALF * jnp.arange(OWN, dtype=jnp.int32)) // inner * inner,
            jnp.stack(
                [
                    offset,
                    jnp.where(odd, 0, chans),
                    jnp.where(odd, 0, chans - extra),
                    jnp.where(odd, slots - 1, 1),
                ]
            ),
            spot ^ jnp.array(relative_order(count, order_b), jnp.int32),
        ]
    ).astype(jnp.int32)

    groups = gate_weight.shape[2] // 16
    group = spot // 2 % groups
    gate_cols = lax.dynamic_slice_in_dim(tie(gate_weight, x_slots[1]), group * 16, 16, 2)
    gate_cols = jnp.transpose(gate_cols, (0, 2, 1, 3)).reshape(2, 16, slots, chans)
    gate_cols = jnp.moveaxis(gate_cols, 2, 0)
    pieces = []
    for k in range(slots):
        piece = lax.dynamic_index_in_dim(gate_cols, (place + k) % slots, 0, keepdims=False)
        if k:
            piece = lax.ppermute(piece, "wshard", [(i, (i + k) % slots) for i in range(slots)])
        pieces.append(piece)
    pieces = [jnp.stack(pieces)]
    for bit in (2, 4):
        pieces = pieces + [exchange_pair(piece, "seq", bit) for piece in pieces]
    rows = inner // slots * ((place - jnp.arange(slots, dtype=jnp.int32)) % slots)
    rows = jnp.stack([rows + 16 * (group ^ (o >> 1)) for o in (0, 2, 4, 6)]).astype(jnp.int32)
    wg = pl.pallas_call(
        assemble_kernel,
        in_specs=[pl.BlockSpec(memory_space=pltpu.SMEM)]
        + [pl.BlockSpec(memory_space=pltpu.VMEM)] * len(pieces),
        out_specs=pl.BlockSpec(memory_space=pltpu.VMEM),
        out_shape=jax.ShapeDtypeStruct((blocks, inner, 2 * HALF), BF16),
    )(rows, *pieces)
    held = ()
    for k in range(slots):
        if 1 <= k < slots - 1:
            x_slots.append(ring(x_slots[k]))
        held = branch_call(x_slots[k], gain_one, w_x, w_y, held, slots, k)
        if k + 1 < slots:
            x_slots[k + 1], *held = join(x_slots[k + 1], *held)
    normed_one, branch_x, branch_y = held
    g_slots = [g_own, ring(tie(g_own, x_slots[-1]))]
    halo = lax.ppermute(
        branch_x[:, tokens - 8 :], "seq", [(i, i + 1) for i in range(count - 1)]
    ).astype(F32)
    wide = jax.ShapeDtypeStruct((slots, tokens, chans), F32)
    low = jax.ShapeDtypeStruct((slots, tokens, chans), BF16)
    pair = jax.ShapeDtypeStruct((slots, 2, chans), F32)
    own_spec = slot_spec(tokens, chans)
    vec_spec = whole_spec((8, chans))
    conv, conv_low, lend = call(
        conv_kernel,
        slots,
        offs,
        (branch_x, halo, conv_vec),
        [own_spec, slot_spec(8, chans), vec_spec],
        (wide, low, jax.ShapeDtypeStruct((slots, tokens, extra), BF16)),
        (own_spec, own_spec, slot_spec(tokens, extra)),
        [pltpu.VMEM((tokens + 8, chans), F32)],
    )
    lent = exchange_pair(lend, "wshard", 1)
    lent, g_slots[1] = join(lent, g_slots[1])
    g_slots.append(ring(g_slots[1]))
    s_rec, s_in, h_local, a_prod, ends, win = call(
        gates_kernel,
        slots,
        offs,
        (conv_low, lent, conv, wg, gate_vec),
        [own_spec, partner_spec(tokens, extra, slots), own_spec, whole_spec(wg.shape), vec_spec],
        (wide,) * 4 + (pair, jax.ShapeDtypeStruct((slots, tokens, window), BF16)),
        (own_spec,) * 4 + (slot_spec(2, chans), slot_spec(tokens, window)),
    )
    scan = prefix_start(ends)
    for bit in bits:
        scan = prefix_step(scan, bit, False)
        if bit == 1:
            *scan, g_slots[2] = join(*scan, g_slots[2])
            g_slots.append(ring(g_slots[2]))
    carry = scan[1][:, 0]
    state = h_local + a_prod * carry[:, None, :]
    gelu_y = gelu_value(branch_y)
    mixed = flat((gelu_y * state.astype(BF16).astype(F32)).astype(BF16))

    out_part, g_slots[3] = join(dot_nn(mixed, w_out), g_slots[3])
    out_slots = split(out_part)
    sent, total = ring_add(out_slots[1], None)
    g_a, g_b = turned([tie(g_slots[0], sent)] + g_slots[1:], (order_a, order_b))
    total, g_a, g_b = join(total, g_a, g_b)
    sent, total = ring_add(out_slots[2], total)
    one_a, one_b = turned([tie(normed_one, sent)], (order_a, order_b))
    x_all = jnp.concatenate([tie(x_own, sent)] + x_slots[1:], axis=0)
    total, one_a, one_b, x_all = join(total, one_a, one_b, x_all)
    _, total = ring_add(out_slots[3], total)
    residual = x_own.astype(F32) + out_slots[0] + total.astype(F32)
    res_scale = rms_scale(residual)
    res_hat = residual * res_scale

    two = [(res_hat * gain_two).astype(BF16)]
    held, total, sent = (), None, None
    for k in range(slots):
        if k + 1 < slots:
            two.append(ring(two[k]))
        here = two[k] if sent is None else tie(two[k], sent)
        *held, part = ffn_call(
            here, g_slots[k], w_gate, w_up, w_down, held, slots, k, BF16 if k == 1 else F32
        )
        if k == 0:
            part_0 = part
            two[1], part = join(two[1], part)
        else:
            if total is not None:
                total, part = join(total, part)
            sent, total = ring_add(part, total)
    act, grad_gate, grad_up = held

    two_a, two_b = turned([tie(two[0], sent)] + two[1:], (order_a, order_b))
    gate_grad = Halving(two_a, grad_gate, order_a)
    up_grad = Halving(two_b, grad_up, order_b)
    cut = act.shape[1] // 2 // HALF * HALF
    down_a = Halving(g_a, act[:, :cut], order_a)
    down_b = Halving(g_b, act[:, cut:], order_b)
    total, half_gate, half_up = join(total, gate_grad.give(), up_grad.give())
    grad_two = part_0 + total.astype(F32)
    gate_grad.send(half_gate)
    up_grad.send(half_up)

    scaled = grad_two * gain_two
    grad_residual = g_own.astype(F32) + res_scale * (
        scaled - res_hat * jnp.mean(scaled * res_hat, axis=-1, keepdims=True)
    )
    grad_norm2 = jnp.sum(grad_two * res_hat, axis=0)
    proj = [grad_residual.astype(BF16)]
    proj.append(ring(proj[0]))
    proj[1], half_a, half_b, half_gate, half_up = join(
        proj[1],
        down_a.give(proj[0]),
        down_b.give(proj[0]),
        gate_grad.give(proj[0]),
        up_grad.give(proj[0]),
    )
    proj.append(ring(proj[1]))
    gate_grad.send(half_gate)
    up_grad.send(half_up)
    down_a.send(half_a)
    down_b.send(half_b)
    proj[2], mlp_part = join(proj[2], dot_nn(tie(act, proj[1]), w_down))
    down_slots = split(mlp_part)
    proj.append(ring(proj[2]))
    proj[3], half_a, half_b = join(proj[3], down_a.give(proj[2]), down_b.give(proj[2]))
    grad_proj = jnp.concatenate(proj, axis=0)
    _, mlp = ring_add(tie(down_slots[1], proj[3]), None)

    grad_mixed = by_slot(dot_nt(grad_proj, w_out))
    grad_y, c_local, c_prod, back_ends = call(
        back_scan_kernel,
        slots,
        offs,
        (grad_mixed, branch_y, state, s_rec, gate_vec),
        [own_spec] * 4 + [vec_spec],
        (low, wide, wide, pair),
        (own_spec,) * 3 + (slot_spec(2, chans),),
    )
    scan = prefix_start(back_ends)
    for bit in bits:
        scan = prefix_step(scan, bit, True)
        if bit == 1:
            *scan, mlp, gate_grad.held[-1], up_grad.held[-1] = join(
                *scan, mlp, gate_grad.held[-1], up_grad.held[-1]
            )
    scan, half_gate, half_up = join(scan[1], gate_grad.give(), up_grad.give())
    gate_grad.send(half_gate)
    up_grad.send(half_up)
    edges = jnp.stack([carry, scan[:, 0]], axis=1)
    pieces = (2 * inner * blocks, HALF)
    whole_pieces = inner // slots // count % 8 != 0
    if whole_pieces:
        pieces = wg.shape
    near, far, gate_parts, gate_sums = call(
        functools.partial(back_gates_kernel, count=count, planes=slots),
        slots,
        offs,
        (c_local, c_prod, edges, s_rec, s_in, conv, state, win, wg, gate_vec),
        [own_spec] * 2
        + [slot_spec(2, chans)]
        + [own_spec] * 4
        + [slot_spec(tokens, window), whole_spec(wg.shape), vec_spec],
        (
            wide,
            jax.ShapeDtypeStruct((slots, tokens, extra), F32),
            jax.ShapeDtypeStruct(pieces, F32),
            jax.ShapeDtypeStruct((8, chans), F32),
        ),
        (own_spec, slot_spec(tokens, extra), whole_spec(pieces), vec_spec),
        [pltpu.VMEM(wg.shape, F32), pltpu.VMEM((tokens, window), F32)],
    )
    if whole_pieces:
        gate_parts = gate_parts.reshape(blocks, slots, count, -1, 2, HALF)
        gate_parts = jnp.transpose(gate_parts, (2, 1, 4, 0, 3, 5))
        gate_parts = jnp.concatenate(
            [
                lax.dynamic_index_in_dim(gate_parts, spot ^ o, 0, keepdims=False)
                for o in relative_order(count, order_b)
            ]
        ).reshape(-1, HALF)
    got = exchange_pair(far, "wshard", 1)
    (proj_a,) = turned([tie(grad_proj, far)], (order_a,))
    out_grad = Halving(proj_a, mixed, order_a)
    y_grad = Halving(one_b, flat(grad_y), order_b, extra=gate_parts)
    got, half_out, half_y, gate_grad.held[-1], up_grad.held[-1] = join(
        got, out_grad.give(), y_grad.give(far), gate_grad.held[-1], up_grad.held[-1]
    )
    out_grad.send(half_out)
    y_grad.send(half_y)
    lent_rows = jnp.concatenate([got[:, :8], got[:, :8]], axis=0)
    lent_rows = lax.dynamic_slice_in_dim(lent_rows, jnp.where(odd, slots - 1, 1), slots, 0)
    blank = jnp.zeros((slots, 8, chans - extra), F32)
    head = near[:, :8] + jnp.where(
        odd,
        jnp.concatenate([lent_rows, blank], axis=2),
        jnp.concatenate([blank, lent_rows], axis=2),
    )
    after = lax.ppermute(head, "seq", [(i + 1, i) for i in range(count - 1)])
    after, half_y, half_out = join(after, y_grad.give(head), out_grad.give(head))
    y_grad.send(half_y)
    out_grad.send(half_out)
    grad_x, conv_sums = call(
        back_conv_kernel,
        slots,
        offs,
        (near, got, after, branch_x, halo, conv_vec),
        [
            own_spec,
            partner_spec(tokens, extra, slots),
            slot_spec(8, chans),
            own_spec,
            slot_spec(8, chans),
            vec_spec,
        ],
        (low, jax.ShapeDtypeStruct((8, chans), F32)),
        (own_spec, vec_spec),
        [pltpu.VMEM((tokens + 8, chans), F32), pltpu.VMEM((tokens + 8, chans), F32)],
    )
    one_part = dot_nn(flat(grad_x), w_x) + dot_nn(flat(grad_y), w_y)
    one_slots = split(one_part)
    sent, total = ring_add(one_slots[1], None)

    down_a.send(tie(half_a, one_part))
    down_b.send(tie(half_b, one_part))
    x_grad = Halving(one_a, flat(grad_x), order_a)
    total, norm1, half_x, y_grad.held[-1], out_grad.held[-1] = join(
        total,
        norm_grad(tie(x_all, sent), one_part, slots),
        x_grad.give(sent),
        y_grad.held[-1],
        out_grad.held[-1],
    )
    sent, total = ring_add(one_slots[2], total)
    x_grad.send(half_x)
    norms = jnp.concatenate([norm1, grad_norm2[None]], axis=0)
    other = exchange_pair(norms, "wshard", 1)

    total, other, half_x, half_y, half_out, down_a.held[-1], down_b.held[-1] = join(
        total,
        other,
        x_grad.give(sent),
        y_grad.give(sent),
        out_grad.give(sent),
        down_a.held[-1],
        down_b.held[-1],
    )
    sent, total = ring_add(one_slots[3], total)
    x_grad.send(half_x)
    y_grad.send(half_y)
    out_grad.send(half_out)
    norms = norms + other
    other = exchange_pair(norms, "wshard", 2)

    total, other, grad_w_gate, half_a, half_b, y_grad.held[-1], out_grad.held[-1] = join(
        total,
        other,
        *gate_grad.finish(sent),
        down_a.give(sent),
        down_b.give(sent),
        y_grad.held[-1],
        out_grad.held[-1],
    )
    sent, mlp = ring_add(down_slots[2], tie(mlp, total))
    down_a.send(half_a)
    down_b.send(half_b)
    norms = lax.dynamic_slice_in_dim(norms + other, place * chans, chans, 1)
    smalls = jnp.concatenate([norms, gate_sums[:3], conv_sums[:5]], axis=0)
    other = exchange_pair(smalls, "seq", bits[0])
    grad_one = one_slots[0] + total.astype(F32)
    own_f = x_own.astype(F32)
    own_scale = rms_scale(own_f)
    own_hat = own_f * own_scale
    scaled_one = grad_one * gain_one
    grad_input = grad_residual + own_scale * (
        scaled_one - own_hat * jnp.mean(scaled_one * own_hat, axis=-1, keepdims=True)
    )
    grad_w_y, gate_parts = y_grad.finish(sent)
    mlp, other, grad_input, grad_w_y, grad_w_up, gate_parts, x_grad.held[-1] = join(
        mlp, other, grad_input, grad_w_y, *up_grad.finish(sent), gate_parts, x_grad.held[-1]
    )
    sent, mlp = ring_add(down_slots[3], mlp)
    smalls = smalls + other
    for bit in bits[1:]:
        smalls = smalls + exchange_pair(smalls, "seq", bit)

    gate_parts = swap_parts(gate_parts.reshape(slots, -1, HALF).astype(BF16))[None]
    for bit in order_b[::-1]:
        gate_parts = jnp.concatenate([gate_parts, exchange_pair(gate_parts, "seq", bit)], axis=0)
    gate_parts = jnp.stack(
        [
            lax.dynamic_index_in_dim(gate_parts, at, 0, keepdims=False)
            for at in [rank_of(j ^ spot, order_b) for j in range(count)]
        ]
    ).astype(F32)
    gate_parts = gate_parts.reshape(count, slots, 2, blocks, -1, HALF)
    gate_parts = jnp.transpose(gate_parts, (2, 0, 4, 1, 3, 5)).reshape(2, -1, heads, inner)
    grad_gates = jnp.transpose(gate_parts, (0, 2, 1, 3))
    (grad_w_x,) = x_grad.finish(sent)
    (grad_w_out,) = out_grad.finish(sent)
    grad_w_down = jnp.concatenate([*down_a.finish(sent), *down_b.finish(sent)], axis=0)
    block_out = (residual + down_slots[0] + mlp.astype(F32)).astype(BF16)

    return (
        block_out[None],
        grad_input[None],
        grad_w_x,
        grad_w_y,
        grad_w_out,
        grad_w_gate,
        grad_w_up,
        grad_w_down,
        smalls[0],
        smalls[1],
        smalls[5:9],
        smalls[9],
        grad_gates,
        smalls[3:5],
        DECAY_SCALE * jax.nn.sigmoid(-decay) * smalls[2],
    )


def solution(mesh):
    row = P("wshard", None)
    vec = P("wshard")
    tok = P("wshard", "seq", None)
    grad = P("wshard", "seq")
    return jax.shard_map(
        on_device,
        mesh=mesh,
        in_specs=(
            tok,
            tok,
            row,
            row,
            row,
            row,
            row,
            row,
            vec,
            vec,
            P(None, "wshard"),
            vec,
            P(None, None, "wshard", None),
            P(None, "wshard"),
            vec,
        ),
        out_specs=(
            tok,
            tok,
            grad,
            grad,
            grad,
            grad,
            grad,
            grad,
            vec,
            vec,
            P(None, "wshard"),
            vec,
            P(None, None, "wshard", None),
            P(None, "wshard"),
            vec,
        ),
        check_vma=False,
    )
```

```python
import functools

import jax
import jax.numpy as jnp
from jax import lax
from jax.experimental import pallas as pl
from jax.experimental.pallas import tpu as pltpu
from jax.sharding import PartitionSpec as P

EPS = 1e-06
DECAY_SCALE = 8.0
HALF = 128
GELU_C = 0.7978845608028654
GELU_K = 0.044715
F32 = jnp.float32
BF16 = jnp.bfloat16
OWN, FAR, LEND, SLOT, REL = 16, 17, 18, 19, 20


def ring(value, axis="wshard"):
    count = lax.axis_size(axis)
    return lax.ppermute(value, axis, [(i, (i + 1) % count) for i in range(count)])


def ring_gather(part, axis="wshard"):
    slots = [part]
    for _ in range(1, lax.axis_size(axis)):
        slots.append(ring(slots[-1], axis))
    return slots


def join(*values):
    return lax.optimization_barrier(values)


def ring_add(slot, total, axis="wshard"):
    mine = slot if total is None else slot.astype(F32) + total.astype(F32)
    mine = mine.astype(BF16)
    return mine, ring(mine, axis)


def ring_scatter(slots, axis="wshard"):
    total = None
    for slot in slots[1:]:
        _, total = ring_add(slot, total, axis)
    return slots[0] + total.astype(F32)


def tie(value, *others):
    return lax.optimization_barrier((value,) + others)[0]


def exchange_pair(value, axis, bit):
    count = lax.axis_size(axis)
    return lax.ppermute(value, axis, [(i, i ^ bit) for i in range(count)])


def bits_of(count):
    return [1 << i for i in range(count.bit_length() - 1)]


def sum_all(value, axis):
    for bit in bits_of(lax.axis_size(axis)):
        value = value + exchange_pair(value, axis, bit)
    return value


def from_slots(slots, axis="wshard"):
    count = lax.axis_size(axis)
    place = lax.axis_index(axis)
    back = jnp.stack(slots[::-1] + slots[::-1])
    return lax.dynamic_slice_in_dim(back, count - 1 - place, count, 0)


def all_parts(part, axis="wshard"):
    count = lax.axis_size(axis)
    slots = [part] + [
        lax.ppermute(part, axis, [(i, (i + k) % count) for i in range(count)])
        for k in range(1, count)
    ]
    return from_slots(slots, axis)


def swap_parts(parts, axis="wshard"):
    count = lax.axis_size(axis)
    place = lax.axis_index(axis)
    slots = []
    for k in range(count):
        mine = lax.dynamic_index_in_dim(parts, (place + k) % count, 0, keepdims=False)
        if k:
            mine = lax.ppermute(mine, axis, [(i, (i + k) % count) for i in range(count)])
        slots.append(mine)
    return from_slots(slots, axis)


def relative_order(count, order):
    offsets = [0]
    for bit in reversed(order):
        offsets = offsets + [o | bit for o in offsets]
    return offsets


def prefix_step(state, bit, back, axis="seq"):
    total, before = state
    other = exchange_pair(total, axis, bit)
    high = (lax.axis_index(axis) & bit) != 0
    first = high != back
    before = jnp.stack(
        [
            jnp.where(first, before[:, 0] + before[:, 1] * other[:, 0], before[:, 0]),
            jnp.where(first, before[:, 1] * other[:, 1], before[:, 1]),
        ],
        axis=1,
    )
    total = jnp.stack(
        [
            jnp.where(
                first,
                total[:, 0] + total[:, 1] * other[:, 0],
                other[:, 0] + other[:, 1] * total[:, 0],
            ),
            total[:, 1] * other[:, 1],
        ],
        axis=1,
    )
    return total, before


def prefix_start(ends):
    ones = jnp.ones_like(ends[:, 0])
    return ends, jnp.stack([jnp.zeros_like(ones), ones], axis=1)


def rank_of(offset, order):
    rank = jnp.int32(0)
    for i, bit in enumerate(order):
        rank = rank + jnp.where((offset & bit) != 0, 1 << (len(order) - 1 - i), 0)
    return rank


def turn_kernel(at_ref, *refs, slots):
    outs, held_ref = refs[slots:-1], refs[-1]
    row = 0
    for ref in refs[:slots]:
        for col in range(0, ref.shape[1], HALF):
            held_ref[col : col + HALF, row : row + ref.shape[0]] = ref[:, col : col + HALF].T
        row += ref.shape[0]
    count = at_ref.shape[1]
    width = held_ref.shape[0] // count
    for out, ref in enumerate(outs):
        for q in range(count):
            start = pl.multiple_of(at_ref[out, q], 16)
            ref[q * width : (q + 1) * width] = held_ref[pl.ds(start, width)]


def turned(parts, orders, axis="seq"):
    count = lax.axis_size(axis)
    place = lax.axis_index(axis)
    model = parts[0].shape[1]
    rows = sum(part.shape[0] for part in parts)
    width = model // count
    at = [(place ^ jnp.array(relative_order(count, order), jnp.int32)) * width for order in orders]
    vmem = pl.BlockSpec(memory_space=pltpu.VMEM)
    return pl.pallas_call(
        functools.partial(turn_kernel, slots=len(parts)),
        in_specs=[pl.BlockSpec(memory_space=pltpu.SMEM)] + [vmem] * len(parts),
        out_specs=(vmem,) * len(orders),
        out_shape=(jax.ShapeDtypeStruct((model, rows), parts[0].dtype),) * len(orders),
        scratch_shapes=[pltpu.VMEM((model, rows), parts[0].dtype)],
    )(jnp.stack(at).astype(jnp.int32), *parts)


class Halving:
    def __init__(self, left, right, order, extra=None, axis="seq"):
        self.left, self.right, self.order, self.axis = left, right, list(order), axis
        self.extra = extra
        self.held = []
        self.size = left.shape[0]

    def part(self, lo, hi, after):
        width = self.right.shape[1]
        right = tie(self.right, *after) if after else self.right
        total = dot_nn(self.left[lo:hi], right)
        for piece in self.held:
            total = total + piece[lo:hi, :width].astype(F32)
        if self.extra is None:
            return total, None
        more = self.extra[lo:hi]
        for piece in self.held:
            more = more + piece[lo:hi, width:].astype(F32)
        return total, more

    def give(self, *after):
        total, more = self.part(self.size // 2, self.size, after)
        total = total.astype(BF16)
        return total if more is None else jnp.concatenate([total, more.astype(BF16)], axis=1)

    def send(self, half):
        self.held.append(exchange_pair(half, self.axis, self.order.pop(0)))
        self.size //= 2

    def finish(self, *after):
        while self.order:
            self.send(self.give(*after))
        total, more = self.part(0, self.size, after)
        return (total.T,) if more is None else (total.T, more)


def norm_kernel(x_ref, part_ref, out_ref):
    @pl.when(pl.program_id(0) == 0)
    def _():
        out_ref[...] = jnp.zeros_like(out_ref)

    values = x_ref[...].astype(F32)
    out_ref[...] += jnp.sum(part_ref[...] * (values * rms_scale(values)), axis=0, keepdims=True)


def norm_grad(x, part, slots):
    spec = pl.BlockSpec((x.shape[0] // slots, x.shape[1]), lambda i: (i, 0))
    return pl.pallas_call(
        norm_kernel,
        grid=(slots,),
        in_specs=[spec, spec],
        out_specs=pl.BlockSpec((1, x.shape[1]), lambda i: (0, 0)),
        out_shape=jax.ShapeDtypeStruct((1, x.shape[1]), F32),
    )(x, part)


def expm1_neg(v):
    poly = 1.0 + v / 9.0
    for n in range(8, 1, -1):
        poly = 1.0 + poly * v / float(n)
    return jnp.where(v > -0.5, v * poly, jnp.exp(v) - 1.0)


def gelu_parts(v):
    t = jnp.tanh(GELU_C * (v + GELU_K * v * v * v))
    value = 0.5 * v * (1.0 + t)
    slope = 0.5 * (1.0 + t) + 0.5 * v * (1.0 - t * t) * GELU_C * (1.0 + 3.0 * GELU_K * v * v)
    return value, slope


def gelu_value(v):
    return 0.5 * v * (1.0 + jnp.tanh(GELU_C * (v + GELU_K * v * v * v)))


def row_ids(shape):
    return lax.broadcasted_iota(jnp.int32, shape, 0)


def shift_down(v, k, fill, rows):
    count = v.shape[0]
    if k % 8 == 0:
        return jnp.concatenate([jnp.full((k, v.shape[1]), fill, F32), v[: count - k]], axis=0)
    return jnp.where(rows < k, fill, pltpu.roll(v, k, 0))


def shift_up(v, k, fill, rows):
    count = v.shape[0]
    if k % 8 == 0:
        return jnp.concatenate([v[k:], jnp.full((k, v.shape[1]), fill, F32)], axis=0)
    return jnp.where(rows >= count - k, fill, pltpu.roll(v, count - k, 0))


def run_scan(decay, value, shift, rows):
    k = 1
    while k < value.shape[0]:
        value = value + decay * shift(value, k, 0.0, rows)
        decay = decay * shift(decay, k, 1.0, rows)
        k *= 2
    return decay, value


def assemble_kernel(at_ref, *refs):
    out_ref = refs[-1]
    for i, ref in enumerate(refs[:-1]):
        for j in range(ref.shape[0]):
            row = pl.multiple_of(at_ref[i, j], 16)
            for m in range(out_ref.shape[0]):
                for g in range(2):
                    out_ref[m, pl.ds(row, 16), g * HALF : (g + 1) * HALF] = ref[
                        j, g, :, m * HALF : (m + 1) * HALF
                    ]


def branch_kernel(x_ref, gain_ref, wx_ref, wy_ref, *refs):
    n_ref, bx_ref, by_ref = refs[-3:]
    values = x_ref[...].astype(F32)
    low = (values * rms_scale(values) * gain_ref[...]).astype(BF16)
    n_ref[...] = low
    bx_ref[0] = dot_nt(low, wx_ref[...]).astype(BF16)
    by_ref[0] = dot_nt(low, wy_ref[...])


def branch_call(x, gain, w_x, w_y, held, slots, place):
    rows, model = x.shape
    chans = w_x.shape[0]
    kept = pl.BlockSpec(memory_space=pl.ANY)
    whole = lambda shape: pl.BlockSpec(shape, lambda i: (0,) * len(shape))
    out = pl.BlockSpec((1, rows, chans), lambda i: (place, 0, 0))
    return pl.pallas_call(
        branch_kernel,
        grid=(1,),
        in_specs=[whole(x.shape), whole(gain.shape), whole(w_x.shape), whole(w_y.shape)]
        + [kept] * len(held),
        out_specs=(pl.BlockSpec((rows, model), lambda i: (place, 0)), out, out),
        out_shape=(
            jax.ShapeDtypeStruct((slots * rows, model), BF16),
            jax.ShapeDtypeStruct((slots, rows, chans), BF16),
            jax.ShapeDtypeStruct((slots, rows, chans), F32),
        ),
        input_output_aliases={4 + i: i for i in range(len(held))},
    )(x, gain, w_x, w_y, *held)


def conv_kernel(off_ref, bx_ref, halo_ref, vec_ref, conv_ref, low_ref, lend_ref, ext_ref):
    tokens = bx_ref.shape[1]
    ext_ref[0:8] = halo_ref[0]
    ext_ref[8:] = bx_ref[0].astype(F32)
    total = vec_ref[4:5] + jnp.zeros((tokens, bx_ref.shape[2]), F32)
    for k in range(4):
        total = total + vec_ref[k : k + 1] * ext_ref[8 - k : 8 - k + tokens]
    conv_ref[0] = total
    low_ref[0] = total.astype(BF16)
    lend_ref[0] = low_ref[0, :, pl.ds(pl.multiple_of(off_ref[LEND], HALF), lend_ref.shape[2])]


def gates_kernel(
    off_ref, low_ref, lent_ref, conv_ref, wg_ref, vec_ref,
    s0_ref, s1_ref, h_ref, a_ref, end_ref, win_ref,
):
    tokens = win_ref.shape[1]
    rows = row_ids((tokens, HALF))
    own = pl.multiple_of(off_ref[OWN], HALF)
    far = pl.multiple_of(off_ref[FAR], HALF)
    win_ref[0, :, pl.ds(own, low_ref.shape[2])] = low_ref[0]
    win_ref[0, :, pl.ds(far, lent_ref.shape[2])] = lent_ref[0]
    for m in range(wg_ref.shape[0]):
        cols = slice(m * HALF, (m + 1) * HALF)
        src = pl.multiple_of(off_ref[m], HALF)
        logits = jnp.dot(
            win_ref[0, :, pl.ds(src, 2 * HALF)], wg_ref[m], preferred_element_type=F32
        )
        s0 = jax.nn.sigmoid(logits[:, :HALF] + vec_ref[0:1, cols])
        s1 = jax.nn.sigmoid(logits[:, HALF:] + vec_ref[1:2, cols])
        log_a = vec_ref[2:3, cols] * s0
        value = jnp.sqrt(-expm1_neg(2.0 * log_a)) * (conv_ref[0, :, cols] * s1)
        decay, state = run_scan(jnp.exp(log_a), value, shift_down, rows)
        s0_ref[0, :, cols] = s0
        s1_ref[0, :, cols] = s1
        h_ref[0, :, cols] = state
        a_ref[0, :, cols] = decay
        end_ref[0, 0:1, cols] = state[tokens - 1 :]
        end_ref[0, 1:2, cols] = decay[tokens - 1 :]


def back_scan_kernel(
    off_ref, gm_ref, by_ref, st_ref, s0_ref, vec_ref, gy_ref, c_ref, a_ref, end_ref
):
    tokens = gm_ref.shape[1]
    rows = row_ids((tokens, HALF))
    for m in range(gm_ref.shape[2] // HALF):
        cols = slice(m * HALF, (m + 1) * HALF)
        gm = gm_ref[0, :, cols]
        value, slope = gelu_parts(by_ref[0, :, cols])
        low = st_ref[0, :, cols].astype(BF16).astype(F32)
        gy_ref[0, :, cols] = (gm * low * slope).astype(BF16)
        grad = (gm * value).astype(BF16).astype(F32)
        decay = jnp.exp(vec_ref[2:3, cols] * s0_ref[0, :, cols])
        prod, carried = run_scan(shift_up(decay, 1, 1.0, rows), grad, shift_up, rows)
        c_ref[0, :, cols] = carried
        a_ref[0, :, cols] = prod
        end_ref[0, 0:1, cols] = decay[0:1] * carried[0:1]
        end_ref[0, 1:2, cols] = decay[0:1] * prod[0:1]


def back_gates_kernel(
    off_ref,
    c_ref,
    a_ref,
    edge_ref,
    s0_ref,
    s1_ref,
    conv_ref,
    st_ref,
    win_ref,
    wg_ref,
    vec_ref,
    near_ref,
    far_ref,
    piece_ref,
    sum_ref,
    dw_ref,
    gc_ref,
    *,
    count,
    planes,
):
    tokens = c_ref.shape[1]
    rows = row_ids((tokens, HALF))

    @pl.when(pl.program_id(0) == 0)
    def _():
        dw_ref[...] = jnp.zeros_like(dw_ref)
        sum_ref[...] = jnp.zeros_like(sum_ref)

    gc_ref[...] = jnp.zeros_like(gc_ref)
    for m in range(wg_ref.shape[0]):
        cols = slice(m * HALF, (m + 1) * HALF)
        src = pl.multiple_of(off_ref[m], HALF)
        own = pl.multiple_of(off_ref[OWN] + m * HALF, HALF)
        carried = c_ref[0, :, cols] + a_ref[0, :, cols] * edge_ref[0, 1:2, cols]
        before = shift_down(st_ref[0, :, cols], 1, 0.0, rows)
        before = jnp.where(rows == 0, edge_ref[0, 0:1, cols], before)
        s0 = s0_ref[0, :, cols]
        s1 = s1_ref[0, :, cols]
        conv = conv_ref[0, :, cols]
        coef = vec_ref[2:3, cols]
        log_a = coef * s0
        root = jnp.sqrt(-expm1_neg(2.0 * log_a))
        g_log = carried * (jnp.exp(log_a) * before - jnp.exp(2.0 * log_a) * (conv * s1) / root)
        g_log = g_log.astype(BF16).astype(F32)
        g_in = (carried * root).astype(BF16).astype(F32)
        rec = (g_log * coef * s0 * (1.0 - s0)).astype(BF16)
        inp = (g_in * conv * s1 * (1.0 - s1)).astype(BF16)
        sum_ref[0:1, cols] += jnp.sum(g_log * s0, axis=0, keepdims=True)
        sum_ref[1:2, cols] += jnp.sum(rec.astype(F32), axis=0, keepdims=True)
        sum_ref[2:3, cols] += jnp.sum(inp.astype(F32), axis=0, keepdims=True)
        both = jnp.concatenate([rec, inp], axis=1)
        gc_ref[:, pl.ds(src, 2 * HALF)] += lax.dot_general(
            both, wg_ref[m], (((1,), (1,)), ((), ())), preferred_element_type=F32
        )
        gc_ref[:, pl.ds(own, HALF)] += g_in * s1
        dw_ref[m] += lax.dot_general(
            win_ref[0, :, pl.ds(src, 2 * HALF)],
            both,
            (((0,), (0,)), ((), ())),
            preferred_element_type=F32,
        )

    own = pl.multiple_of(off_ref[OWN], HALF)
    far = pl.multiple_of(off_ref[FAR], HALF)
    near_ref[0] = gc_ref[:, pl.ds(own, near_ref.shape[2])]
    far_ref[0] = gc_ref[:, pl.ds(far, far_ref.shape[2])].astype(BF16)

    @pl.when(pl.program_id(0) == pl.num_programs(0) - 1)
    def _():
        blocks = dw_ref.shape[0]
        width = dw_ref.shape[1] // (planes * count)
        if width % 8:
            piece_ref[...] = dw_ref[...]
            return
        row = 0
        for q in range(count):
            for j in range(planes):
                first = pl.multiple_of((j * count + off_ref[REL + q]) * width, width)
                for g in range(2):
                    for m in range(blocks):
                        piece_ref[row : row + width] = dw_ref[
                            m, pl.ds(first, width), g * HALF : (g + 1) * HALF
                        ]
                        row += width


def back_conv_kernel(
    off_ref, gc_ref, got_ref, after_ref, bx_ref, halo_ref, vec_ref, gx_ref, sum_ref, g_ext, x_ext
):
    tokens = gc_ref.shape[1]

    @pl.when(pl.program_id(0) == 0)
    def _():
        sum_ref[...] = jnp.zeros_like(sum_ref)

    lend = pl.multiple_of(off_ref[LEND], HALF)
    g_ext[0:tokens] = gc_ref[0]
    g_ext[0:tokens, pl.ds(lend, got_ref.shape[2])] += got_ref[0].astype(F32)
    grad = g_ext[0:tokens]
    g_ext[tokens:] = after_ref[0]
    x_ext[0:8] = halo_ref[0]
    x_ext[8:] = bx_ref[0].astype(F32)
    total = jnp.zeros_like(grad)
    for k in range(4):
        total = total + vec_ref[k : k + 1] * g_ext[k : k + tokens]
        sum_ref[k : k + 1] += jnp.sum(
            grad * x_ext[8 - k : 8 - k + tokens], axis=0, keepdims=True
        )
    sum_ref[4:5] += jnp.sum(grad, axis=0, keepdims=True)
    gx_ref[0] = total.astype(BF16)


def ffn_kernel(two_ref, g_ref, wg_ref, wu_ref, wd_ref, *refs):
    act_ref, gate_ref, up_ref, part_ref, total_ref = refs[-5:]
    step = pl.program_id(0)
    gate = dot_nt(two_ref[...], wg_ref[...])
    up = dot_nt(two_ref[...], wu_ref[...])
    grad = dot_nt(g_ref[...], wd_ref[...])
    value, slope = gelu_parts(gate)
    act_ref[...] = (value * up).astype(BF16)
    grad_gate = (grad * up * slope).astype(BF16)
    grad_up = (grad * value).astype(BF16)
    gate_ref[...] = grad_gate
    up_ref[...] = grad_up
    part = dot_nn(grad_gate, wg_ref[...]) + dot_nn(grad_up, wu_ref[...])

    @pl.when(step == 0)
    def _():
        total_ref[...] = part

    @pl.when(step > 0)
    def _():
        total_ref[...] += part

    @pl.when(step == pl.num_programs(0) - 1)
    def _():
        part_ref[...] = total_ref[...].astype(part_ref.dtype)


def ffn_call(two, grad, w_gate, w_up, w_down, held, slots, place, kind):
    rows, model = two.shape
    hidden = w_gate.shape[0]
    width = next(w for w in (384, 256, HALF) if hidden % w == 0)
    tok = pl.BlockSpec((rows, model), lambda i: (0, 0))
    weight = pl.BlockSpec((width, model), lambda i: (i, 0))
    wide = pl.BlockSpec((rows, width), lambda i: (place, i))
    kept = pl.BlockSpec(memory_space=pl.ANY)
    return pl.pallas_call(
        ffn_kernel,
        grid=(hidden // width,),
        in_specs=[tok, tok, weight, weight, weight] + [kept] * len(held),
        out_specs=(wide,) * 3 + (tok,),
        out_shape=(jax.ShapeDtypeStruct((slots * rows, hidden), BF16),) * 3
        + (jax.ShapeDtypeStruct((rows, model), kind),),
        scratch_shapes=[pltpu.VMEM((rows, model), F32)],
        input_output_aliases={5 + i: i for i in range(len(held))},
    )(two, grad, w_gate, w_up, w_down, *held)


def gate_out_kernel(off_ref, in_ref, out_ref):
    count, planes, rows = in_ref.shape[:3]
    per = out_ref.shape[3] // HALF
    blocks = out_ref.shape[1] * per // planes
    width = rows // (2 * blocks)
    for r in range(count):
        row = pl.multiple_of(off_ref[REL + r] * width, width)
        for j in range(planes):
            values = in_ref[r, j].astype(F32)
            for g in range(2):
                for m in range(blocks):
                    at = blocks * j + m
                    first = (g * blocks + m) * width
                    cols = slice(at % per * HALF, (at % per + 1) * HALF)
                    out_ref[g, at // per, pl.ds(row, width), cols] = values[first : first + width]


def slot_spec(rows, width):
    return pl.BlockSpec((1, rows, width), lambda i, off: (i, 0, 0))


def partner_spec(rows, width, slots):
    return pl.BlockSpec((1, rows, width), lambda i, off: ((i + off[SLOT]) % slots, 0, 0))


def whole_spec(shape):
    zero = (0,) * len(shape)
    return pl.BlockSpec(shape, lambda i, off: zero)


def call(kernel, slots, offs, ins, in_specs, outs, out_specs, scratch=()):
    return pl.pallas_call(
        kernel,
        grid_spec=pltpu.PrefetchScalarGridSpec(
            num_scalar_prefetch=1,
            grid=(slots,),
            in_specs=in_specs,
            out_specs=out_specs,
            scratch_shapes=list(scratch),
        ),
        out_shape=outs,
    )(offs, *ins)


def rms_scale(values):
    return lax.rsqrt(jnp.mean(values * values, axis=-1, keepdims=True) + EPS)


def dot_nt(a, b):
    return lax.dot_general(a, b, (((1,), (1,)), ((), ())), preferred_element_type=F32)


def dot_nn(a, b):
    return jnp.dot(a, b, preferred_element_type=F32)


def on_device(
    block_in,
    cotangent,
    w_x,
    w_y,
    w_out,
    w_gate,
    w_up,
    w_down,
    norm1_gain,
    norm2_gain,
    conv_weight,
    conv_bias,
    gate_weight,
    gate_bias,
    decay_param,
):
    slots = lax.axis_size("wshard")
    place = lax.axis_index("wshard")
    count = lax.axis_size("seq")
    spot = lax.axis_index("seq")
    x_own = block_in[0]
    g_own = cotangent[0]
    tokens, model = x_own.shape
    chans = w_x.shape[0]
    heads, inner = gate_weight.shape[1], gate_weight.shape[3]
    taps = conv_weight.shape[0]
    blocks = chans // HALF
    offset = (chans * place) % inner
    window = -(-(chans + (chans % inner)) // inner) * inner
    odd = offset != 0
    bits = bits_of(count)
    order_a = bits
    order_b = bits[:1] + bits[1:][::-1]
    slot_rows = slots * tokens

    def by_slot(v):
        return v.reshape(slots, tokens, v.shape[-1])

    def flat(v):
        return v.reshape(slot_rows, v.shape[-1])

    def split(v):
        return [v[k * tokens : (k + 1) * tokens] for k in range(slots)]

    x_slots = [x_own, ring(x_own)]
    gains = all_parts(tie(jnp.stack([norm1_gain, norm2_gain]), x_slots[1]))
    gains = jnp.swapaxes(gains, 0, 1).reshape(2, model).astype(F32)
    gain_one, gain_two = gains[0:1], gains[1:2]
    conv_vec = jnp.concatenate(
        [conv_weight.astype(F32), conv_bias.astype(F32)[None], jnp.zeros((3, chans), F32)], axis=0
    )
    decay = decay_param.astype(F32)
    coef = -DECAY_SCALE * jax.nn.softplus(-decay)
    gate_vec = jnp.concatenate(
        [gate_bias.astype(F32), coef[None], jnp.zeros((5, chans), F32)], axis=0
    )
    extra = window - chans
    offs = jnp.concatenate(
        [
            (offset + HALF * jnp.arange(OWN, dtype=jnp.int32)) // inner * inner,
            jnp.stack(
                [
                    offset,
                    jnp.where(odd, 0, chans),
                    jnp.where(odd, 0, chans - extra),
                    jnp.where(odd, slots - 1, 1),
                ]
            ),
            spot ^ jnp.array(relative_order(count, order_b), jnp.int32),
        ]
    ).astype(jnp.int32)

    groups = gate_weight.shape[2] // 16
    group = spot // 2 % groups

    def fetch(after):
        gate_cols = lax.dynamic_slice_in_dim(tie(gate_weight, after), group * 16, 16, 2)
        gate_cols = jnp.transpose(gate_cols, (0, 2, 1, 3)).reshape(2, 16, slots, chans)
        gate_cols = jnp.moveaxis(gate_cols, 2, 0)
        pieces = []
        for k in range(slots):
            piece = lax.dynamic_index_in_dim(gate_cols, (place + k) % slots, 0, keepdims=False)
            if k:
                piece = lax.ppermute(piece, "wshard", [(i, (i + k) % slots) for i in range(slots)])
            pieces.append(piece)
        return pieces

    def assemble(pieces):
        pieces = [jnp.stack(pieces)]
        for bit in (2, 4):
            pieces = pieces + [exchange_pair(piece, "seq", bit) for piece in pieces]
        rows = inner // slots * ((place - jnp.arange(slots, dtype=jnp.int32)) % slots)
        rows = jnp.stack([rows + 16 * (group ^ (o >> 1)) for o in (0, 2, 4, 6)]).astype(jnp.int32)
        return pl.pallas_call(
            assemble_kernel,
            in_specs=[pl.BlockSpec(memory_space=pltpu.SMEM)]
            + [pl.BlockSpec(memory_space=pltpu.VMEM)] * len(pieces),
            out_specs=pl.BlockSpec(memory_space=pltpu.VMEM),
            out_shape=jax.ShapeDtypeStruct((blocks, inner, 2 * HALF), BF16),
        )(rows, *pieces)

    held = ()
    for k in range(slots):
        if 1 <= k < slots - 1:
            x_slots.append(ring(x_slots[k]))
        if k == slots - 2:
            pieces = fetch(x_slots[k])
        held = branch_call(x_slots[k], gain_one, w_x, w_y, held, slots, k)
        if 1 <= k < slots - 1:
            x_slots[k + 1], *held = join(x_slots[k + 1], *held)
    normed_one, branch_x, branch_y = held
    g_slots = [g_own, ring(tie(g_own, x_slots[-1]))]
    halo = lax.ppermute(
        branch_x[:, tokens - 8 :], "seq", [(i, i + 1) for i in range(count - 1)]
    ).astype(F32)
    wide = jax.ShapeDtypeStruct((slots, tokens, chans), F32)
    low = jax.ShapeDtypeStruct((slots, tokens, chans), BF16)
    pair = jax.ShapeDtypeStruct((slots, 2, chans), F32)
    own_spec = slot_spec(tokens, chans)
    vec_spec = whole_spec((8, chans))
    conv, conv_low, lend = call(
        conv_kernel,
        slots,
        offs,
        (branch_x, halo, conv_vec),
        [own_spec, slot_spec(8, chans), vec_spec],
        (wide, low, jax.ShapeDtypeStruct((slots, tokens, extra), BF16)),
        (own_spec, own_spec, slot_spec(tokens, extra)),
        [pltpu.VMEM((tokens + 8, chans), F32)],
    )
    lend, *pieces = join(lend, *pieces)
    wg = assemble(pieces)
    lent = exchange_pair(lend, "wshard", 1)
    lent, g_slots[1], wg = join(lent, g_slots[1], wg)
    g_slots.append(ring(g_slots[1]))
    s_rec, s_in, h_local, a_prod, ends, win = call(
        gates_kernel,
        slots,
        offs,
        (conv_low, lent, conv, wg, gate_vec),
        [own_spec, partner_spec(tokens, extra, slots), own_spec, whole_spec(wg.shape), vec_spec],
        (wide,) * 4 + (pair, jax.ShapeDtypeStruct((slots, tokens, window), BF16)),
        (own_spec,) * 4 + (slot_spec(2, chans), slot_spec(tokens, window)),
    )
    scan = prefix_start(ends)
    for bit in bits:
        scan = prefix_step(scan, bit, False)
        if bit == 1:
            *scan, g_slots[2] = join(*scan, g_slots[2])
            g_slots.append(ring(g_slots[2]))
    carry = scan[1][:, 0]
    state = h_local + a_prod * carry[:, None, :]
    gelu_y = gelu_value(branch_y)
    mixed = flat((gelu_y * state.astype(BF16).astype(F32)).astype(BF16))

    out_slots = split(dot_nn(mixed, w_out))
    sent, total = ring_add(out_slots[1], None)
    one_a, one_b = turned([tie(normed_one, sent)], (order_a, order_b))
    x_all = jnp.concatenate([tie(x_own, sent)] + x_slots[1:], axis=0)
    total, one_a, one_b, x_all, g_slots[3] = join(total, one_a, one_b, x_all, g_slots[3])
    sent, total = ring_add(out_slots[2], total)
    g_a, g_b = turned([tie(g_slots[0], sent)] + g_slots[1:], (order_a, order_b))
    total, g_a, g_b = join(total, g_a, g_b)
    _, total = ring_add(out_slots[3], total)
    residual = x_own.astype(F32) + out_slots[0] + total.astype(F32)
    res_scale = rms_scale(residual)
    res_hat = residual * res_scale

    two = [(res_hat * gain_two).astype(BF16)]
    held, total, sent = (), None, None
    for k in range(slots):
        if k + 1 < slots:
            two.append(ring(two[k]))
        here = two[k] if sent is None else tie(two[k], sent)
        *held, part = ffn_call(
            here, g_slots[k], w_gate, w_up, w_down, held, slots, k, BF16 if k == 1 else F32
        )
        if k == 0:
            part_0 = part
            two[1], part = join(two[1], part)
        else:
            if total is not None:
                total, part = join(total, part)
            if k + 1 < slots:
                two[k + 1], part = join(two[k + 1], part)
            sent, total = ring_add(part, total)
    act, grad_gate, grad_up = held

    two_a, two_b = turned([tie(two[0], sent)] + two[1:], (order_a, order_b))
    gate_grad = Halving(two_a, grad_gate, order_a)
    up_grad = Halving(two_b, grad_up, order_b)
    cut = act.shape[1] // 2 // HALF * HALF
    down_a = Halving(g_a, act[:, :cut], order_a)
    down_b = Halving(g_b, act[:, cut:], order_b)
    total, half_gate, half_up = join(total, gate_grad.give(), up_grad.give())
    grad_two = part_0 + total.astype(F32)
    gate_grad.send(half_gate)
    up_grad.send(half_up)

    scaled = grad_two * gain_two
    grad_residual = g_own.astype(F32) + res_scale * (
        scaled - res_hat * jnp.mean(scaled * res_hat, axis=-1, keepdims=True)
    )
    grad_norm2 = jnp.sum(grad_two * res_hat, axis=0)
    proj = [grad_residual.astype(BF16)]
    proj.append(ring(proj[0]))
    proj[1], half_a, half_b, half_gate, half_up = join(
        proj[1],
        down_a.give(proj[0]),
        down_b.give(proj[0]),
        gate_grad.give(proj[0]),
        up_grad.give(proj[0]),
    )
    proj.append(ring(proj[1]))
    gate_grad.send(half_gate)
    up_grad.send(half_up)
    down_a.send(half_a)
    down_b.send(half_b)
    proj[2], mlp_part = join(proj[2], dot_nn(tie(act, proj[1]), w_down))
    down_slots = split(mlp_part)
    proj.append(ring(proj[2]))
    proj[3], half_a, half_b = join(proj[3], down_a.give(proj[2]), down_b.give(proj[2]))
    grad_proj = jnp.concatenate(proj, axis=0)
    _, mlp = ring_add(tie(down_slots[1], proj[3]), None)

    grad_mixed = by_slot(dot_nt(grad_proj, w_out))
    grad_y, c_local, c_prod, back_ends = call(
        back_scan_kernel,
        slots,
        offs,
        (grad_mixed, branch_y, state, s_rec, gate_vec),
        [own_spec] * 4 + [vec_spec],
        (low, wide, wide, pair),
        (own_spec,) * 3 + (slot_spec(2, chans),),
    )
    scan = prefix_start(back_ends)
    for bit in bits:
        scan = prefix_step(scan, bit, True)
        if bit == 1:
            *scan, mlp, gate_grad.held[-1], up_grad.held[-1] = join(
                *scan, mlp, gate_grad.held[-1], up_grad.held[-1]
            )
    scan, half_gate, half_up = join(scan[1], gate_grad.give(), up_grad.give())
    gate_grad.send(half_gate)
    up_grad.send(half_up)
    edges = jnp.stack([carry, scan[:, 0]], axis=1)
    pieces = (2 * inner * blocks, HALF)
    whole_pieces = inner // slots // count % 8 != 0
    if whole_pieces:
        pieces = wg.shape
    near, far, gate_parts, gate_sums = call(
        functools.partial(back_gates_kernel, count=count, planes=slots),
        slots,
        offs,
        (c_local, c_prod, edges, s_rec, s_in, conv, state, win, wg, gate_vec),
        [own_spec] * 2
        + [slot_spec(2, chans)]
        + [own_spec] * 4
        + [slot_spec(tokens, window), whole_spec(wg.shape), vec_spec],
        (
            wide,
            jax.ShapeDtypeStruct((slots, tokens, extra), BF16),
            jax.ShapeDtypeStruct(pieces, F32),
            jax.ShapeDtypeStruct((8, chans), F32),
        ),
        (own_spec, slot_spec(tokens, extra), whole_spec(pieces), vec_spec),
        [pltpu.VMEM(wg.shape, F32), pltpu.VMEM((tokens, window), F32)],
    )
    if whole_pieces:
        gate_parts = gate_parts.reshape(blocks, slots, count, -1, 2, HALF)
        gate_parts = jnp.transpose(gate_parts, (2, 1, 4, 0, 3, 5))
        gate_parts = jnp.concatenate(
            [
                lax.dynamic_index_in_dim(gate_parts, spot ^ o, 0, keepdims=False)
                for o in relative_order(count, order_b)
            ]
        ).reshape(-1, HALF)
    got = exchange_pair(far, "wshard", 1)
    (proj_a,) = turned([tie(grad_proj, far)], (order_a,))
    out_grad = Halving(proj_a, mixed, order_a)
    y_grad = Halving(one_b, flat(grad_y), order_b, extra=gate_parts)
    got, half_out, half_y, gate_grad.held[-1], up_grad.held[-1] = join(
        got, out_grad.give(), y_grad.give(far), gate_grad.held[-1], up_grad.held[-1]
    )
    out_grad.send(half_out)
    y_grad.send(half_y)
    lent_rows = jnp.concatenate([got[:, :8], got[:, :8]], axis=0).astype(F32)
    lent_rows = lax.dynamic_slice_in_dim(lent_rows, jnp.where(odd, slots - 1, 1), slots, 0)
    blank = jnp.zeros((slots, 8, chans - extra), F32)
    head = near[:, :8] + jnp.where(
        odd,
        jnp.concatenate([lent_rows, blank], axis=2),
        jnp.concatenate([blank, lent_rows], axis=2),
    )
    after = lax.ppermute(head, "seq", [(i + 1, i) for i in range(count - 1)])
    after, half_y, half_out = join(after, y_grad.give(head), out_grad.give(head))
    y_grad.send(half_y)
    out_grad.send(half_out)
    grad_x, conv_sums = call(
        back_conv_kernel,
        slots,
        offs,
        (near, got, after, branch_x, halo, conv_vec),
        [
            own_spec,
            partner_spec(tokens, extra, slots),
            slot_spec(8, chans),
            own_spec,
            slot_spec(8, chans),
            vec_spec,
        ],
        (low, jax.ShapeDtypeStruct((8, chans), F32)),
        (own_spec, vec_spec),
        [pltpu.VMEM((tokens + 8, chans), F32), pltpu.VMEM((tokens + 8, chans), F32)],
    )
    one_part = dot_nn(flat(grad_x), w_x) + dot_nn(flat(grad_y), w_y)
    one_slots = split(one_part)
    sent, total = ring_add(one_slots[1], None)

    down_a.send(tie(half_a, one_part))
    down_b.send(tie(half_b, one_part))
    x_grad = Halving(one_a, flat(grad_x), order_a)
    total, norm1, half_x, y_grad.held[-1], out_grad.held[-1] = join(
        total,
        norm_grad(tie(x_all, sent), one_part, slots),
        x_grad.give(sent),
        y_grad.held[-1],
        out_grad.held[-1],
    )
    sent, total = ring_add(one_slots[2], total)
    x_grad.send(half_x)
    norms = jnp.concatenate([norm1, grad_norm2[None]], axis=0)
    other = exchange_pair(norms, "wshard", 1)

    total, other, half_x, half_y, half_out = join(
        total, other, x_grad.give(sent), y_grad.give(sent), out_grad.give(sent)
    )
    sent, total = ring_add(one_slots[3], total)
    x_grad.send(half_x)
    y_grad.send(half_y)
    out_grad.send(half_out)
    norms = norms + other
    other = exchange_pair(norms, "wshard", 2)

    total, other, grad_w_gate, *held = join(
        total,
        other,
        *gate_grad.finish(sent),
        y_grad.held[-1],
        out_grad.held[-1],
        down_a.held[-1],
        down_b.held[-1],
    )
    for w, piece in zip((y_grad, out_grad, down_a, down_b), held):
        w.held[-1] = piece
    sent, mlp = ring_add(down_slots[2], tie(mlp, total))
    norms = lax.dynamic_slice_in_dim(norms + other, place * chans, chans, 1)
    smalls = jnp.concatenate([norms, gate_sums[:3], conv_sums[:5]], axis=0)
    other = exchange_pair(smalls, "seq", bits[0])
    grad_one = one_slots[0] + total.astype(F32)
    own_f = x_own.astype(F32)
    own_scale = rms_scale(own_f)
    own_hat = own_f * own_scale
    scaled_one = grad_one * gain_one
    grad_input = grad_residual + own_scale * (
        scaled_one - own_hat * jnp.mean(scaled_one * own_hat, axis=-1, keepdims=True)
    )
    grad_w_y, gate_parts = y_grad.finish(sent)
    mlp, other, grad_input, grad_w_y, half_a, half_b, gate_parts, x_grad.held[-1] = join(
        mlp,
        other,
        grad_input,
        grad_w_y,
        down_a.give(sent),
        down_b.give(sent),
        gate_parts,
        x_grad.held[-1],
    )
    down_a.send(half_a)
    down_b.send(half_b)
    gate_parts = swap_parts(gate_parts.reshape(slots, -1, HALF).astype(BF16))[None]
    gate_parts, mlp = join(gate_parts, mlp)
    sent, mlp = ring_add(down_slots[3], mlp)
    (grad_w_up,) = up_grad.finish(sent)
    smalls = smalls + other
    for bit in bits[1:]:
        smalls = smalls + exchange_pair(smalls, "seq", bit)

    for bit in order_b[::-1]:
        gate_parts = jnp.concatenate([gate_parts, exchange_pair(gate_parts, "seq", bit)], axis=0)
    if whole_pieces:
        gate_parts = jnp.stack(
            [
                lax.dynamic_index_in_dim(gate_parts, at, 0, keepdims=False)
                for at in [rank_of(j ^ spot, order_b) for j in range(count)]
            ]
        ).astype(F32)
        gate_parts = gate_parts.reshape(count, slots, 2, blocks, -1, HALF)
        gate_parts = jnp.transpose(gate_parts, (2, 0, 4, 1, 3, 5)).reshape(2, -1, heads, inner)
        grad_gates = jnp.transpose(gate_parts, (0, 2, 1, 3))
    else:
        grad_gates = pl.pallas_call(
            gate_out_kernel,
            in_specs=[
                pl.BlockSpec(memory_space=pltpu.SMEM),
                pl.BlockSpec(memory_space=pltpu.VMEM),
            ],
            out_specs=pl.BlockSpec(memory_space=pltpu.VMEM),
            out_shape=jax.ShapeDtypeStruct((2, heads, inner // slots, inner), F32),
        )(offs, gate_parts)
    (grad_w_x,) = x_grad.finish(sent)
    (grad_w_out,) = out_grad.finish(sent)
    grad_w_down = jnp.concatenate([*down_a.finish(sent), *down_b.finish(sent)], axis=0)
    block_out = (residual + down_slots[0] + mlp.astype(F32)).astype(BF16)

    return (
        block_out[None],
        grad_input[None],
        grad_w_x,
        grad_w_y,
        grad_w_out,
        grad_w_gate,
        grad_w_up,
        grad_w_down,
        smalls[0],
        smalls[1],
        smalls[5:9],
        smalls[9],
        grad_gates,
        smalls[3:5],
        DECAY_SCALE * jax.nn.sigmoid(-decay) * smalls[2],
    )


def solution(mesh):
    row = P("wshard", None)
    vec = P("wshard")
    tok = P("wshard", "seq", None)
    grad = P("wshard", "seq")
    return jax.shard_map(
        on_device,
        mesh=mesh,
        in_specs=(
            tok,
            tok,
            row,
            row,
            row,
            row,
            row,
            row,
            vec,
            vec,
            P(None, "wshard"),
            vec,
            P(None, None, "wshard", None),
            P(None, "wshard"),
            vec,
        ),
        out_specs=(
            tok,
            tok,
            grad,
            grad,
            grad,
            grad,
            grad,
            grad,
            vec,
            vec,
            P(None, "wshard"),
            vec,
            P(None, None, "wshard", None),
            P(None, "wshard"),
            vec,
        ),
        check_vma=False,
    )
```
